512 devices in a mesh: genome: 128 (over z, y, core), tower: 4 (over x).
Axes of the slice: x: 4, y: 8, z: 8, core: 2. Of those that a mesh axis runs over, the one named last changes fastest.
Arguments:
- genome_bases: int32 [16777216], P('genome'), may hold values from 0 to 3
- stitch_weight: int32 [256], replicated, may hold values from 1 to 8
- stem_weight: bfloat16 [96, 8192], replicated, may hold values from -0.125 to 0.125
- trunk_in: bfloat16 [6, 48, 288], replicated, may hold values from -0.375 to 0.375
- trunk_out: bfloat16 [6, 96, 48], replicated, may hold values from -0.875 to 0.875
- pair_weight: bfloat16 [96, 96], replicated, may hold values from -0.625 to 0.625
- distance_rate: float32 [48], replicated, may hold values from 0.05 to 0.3
- tower_conv: bfloat16 [2, 3, 48, 144], replicated, may hold values from -0.3125 to 0.3125
- tower_mix: bfloat16 [2, 48, 48], replicated, may hold values from -0.875 to 0.875
- head_weight: bfloat16 [5, 48], replicated, may hold values from -0.875 to 0.875
Outputs:
- stitched: float32 [5, 8192, 256], P(None, ('genome', 'tower'))
- scores: float32 [2, 5, 8192], P(None, None, ('genome', 'tower'))
The draws below stay inside these ranges and needn't reach their ends.
All inputs are finite; a program needn't handle non-finite values.
Results may differ from the reference program's by a relative error of at most 0.019.
Values may be sent and summed in bfloat16 or wider, within the bound.
A program may use at most 64 MiB of HBM per device.

```python
import jax
import jax.numpy as jnp
from jax import lax

C1 = 96
MID = 48
C2 = 48
TARGETS = 5
BP = 2048
TRUNK = 6
TOWER = 2
STRIDE = 64
BINS = 256
BASES = 16777216
N_GENOME = 128


def touch_ends(array, own_key, least, largest):
    dims = array.shape
    place = [jax.random.randint(jax.random.fold_in(own_key, axis), (), 0, dims[axis]) for axis in range(len(dims))]
    array = array.at[tuple(place)].set(least)
    longest = dims.index(max(dims))
    place[longest] = (place[longest] + 1) % dims[longest]
    return array.at[tuple(place)].set(largest)


def centred(own_key, shape, spread, most, held_as=jnp.bfloat16):
    drawn = jax.random.normal(own_key, shape, jnp.float32) * spread
    return jnp.minimum(jnp.maximum(drawn, -most), most).astype(held_as)


def setup_inputs(seed: int = 0) -> dict:
    key_of = jax.random.split(jax.random.key(seed), 11)
    return {
        "genome_bases": touch_ends(jax.random.randint(key_of[0], (BASES,), 0, 4), jax.random.fold_in(key_of[0], 1), 0, 3).astype(jnp.int32),
        "stitch_weight": touch_ends(jax.random.randint(key_of[1], (BINS,), 1, 9), jax.random.fold_in(key_of[1], 1), 1, 8).astype(jnp.int32),
        "stem_weight": centred(key_of[2], (C1, 4 * BP), BP ** -0.5, 0.125),
        "trunk_in": centred(key_of[3], (TRUNK, MID, 3 * C1), (3 * C1) ** -0.5, 0.375),
        "trunk_out": centred(key_of[4], (TRUNK, C1, MID), MID ** -0.5, 0.875),
        "pair_weight": centred(key_of[5], (2 * C2, C1), C1 ** -0.5, 0.625),
        "distance_rate": jnp.clip(jax.random.uniform(key_of[6], (C2,), jnp.float32, 0.05, 0.3), 0.05, 0.3),
        "tower_conv": centred(key_of[7], (TOWER, 3, C2, 3 * C2), (9 * C2) ** -0.5, 0.3125),
        "tower_mix": centred(key_of[8], (TOWER, C2, C2), C2 ** -0.5, 0.875),
        "head_weight": centred(key_of[9], (TARGETS, C2), C2 ** -0.5, 0.875),
    }


def shift_cols(values, offset):
    extent = values.shape[-1]
    margins = [(0, 0)] * (values.ndim - 1)
    if offset >= 0:
        padded = jnp.pad(values, margins + [(0, offset)])
        return padded[..., offset:offset + extent]
    padded = jnp.pad(values, margins + [(-offset, 0)])
    return padded[..., :extent]


def stem_features(genome_bases, stem_weight):
    letters = genome_bases.reshape(-1, BP)
    onehot = (letters[:, :, None] == jnp.arange(4, dtype=jnp.int32)[None, None, :]).astype(jnp.bfloat16)
    onehot = onehot.reshape(letters.shape[0], 4 * BP)
    summed = lax.dot_general(stem_weight, onehot, (((1,), (1,)), ((), ())), preferred_element_type=jnp.float32)
    return summed.astype(jnp.bfloat16)


def trunk_stream(window, trunk_in, trunk_out):
    stream = window.astype(jnp.float32)
    layers = trunk_in.shape[0]
    extent = window.shape[-1]
    for layer_index in range(layers):
        dilation = max(1, extent // 2 ** (layers - layer_index))
        active = jax.nn.relu(stream).astype(jnp.bfloat16)
        stacked = jnp.concatenate([shift_cols(active, -dilation), active, shift_cols(active, dilation)], axis=0)
        inner = jnp.dot(trunk_in[layer_index], stacked, preferred_element_type=jnp.float32)
        squeezed = jax.nn.relu(inner).astype(jnp.bfloat16)
        stream = stream + jnp.dot(trunk_out[layer_index], squeezed, preferred_element_type=jnp.float32)
    return stream


def conv_square(active, kernel):
    channels = active.shape[0]
    extent = active.shape[1]
    padded = jnp.pad(active, ((0, 0), (1, 1), (1, 1)))
    summed = jnp.zeros((kernel.shape[1], extent * extent), jnp.float32)
    for row_tap in range(3):
        stacked = jnp.concatenate([padded[:, row_tap:row_tap + extent, col_tap:col_tap + extent] for col_tap in range(3)], axis=0)
        summed = summed + jnp.dot(kernel[row_tap], stacked.reshape(3 * channels, extent * extent), preferred_element_type=jnp.float32)
    return summed.reshape(kernel.shape[1], extent, extent)


def skew_square(contact_maps):
    targets = contact_maps.shape[0]
    extent = contact_maps.shape[1]
    padded = jnp.pad(contact_maps, ((0, 0), (0, 0), (0, extent)))
    flattened = padded.reshape(targets, extent * 2 * extent)
    flattened = jnp.pad(flattened, ((0, 0), (0, extent)))
    sliced = flattened[:, :extent * (2 * extent + 1)]
    return sliced.reshape(targets, extent, 2 * extent + 1)[:, :, :extent]


def reference(genome_bases, stitch_weight, stem_weight, trunk_in, trunk_out, pair_weight, distance_rate, tower_conv, tower_mix, head_weight):
    features = stem_features(genome_bases, stem_weight)
    padded_features = jnp.pad(features, ((0, 0), (0, BINS - STRIDE)))
    row_weight = stitch_weight.astype(jnp.float32)
    channels = distance_rate.shape[0]
    positions = jnp.arange(BINS)
    separation = jnp.abs(positions[:, None] - positions[None, :]).astype(jnp.float32)
    decay_term = jnp.log1p(separation)

    def one_window(window_index):
        window = lax.dynamic_slice_in_dim(padded_features, window_index * STRIDE, BINS, axis=1)
        stream = trunk_stream(window, trunk_in, trunk_out)
        projected = jnp.dot(pair_weight, jax.nn.relu(stream).astype(jnp.bfloat16), preferred_element_type=jnp.float32)
        mixed = projected[:channels][:, :, None] + projected[channels:][:, None, :] - distance_rate[:, None, None] * decay_term[None]
        pair_map = jax.nn.relu(mixed).astype(jnp.bfloat16)
        grid = pair_map.astype(jnp.float32)
        for layer_index in range(TOWER):
            active = jax.nn.relu(grid).astype(jnp.bfloat16)
            convolved = conv_square(active, tower_conv[layer_index])
            squeezed = jax.nn.relu(convolved).astype(jnp.bfloat16)
            update = jnp.dot(tower_mix[layer_index], squeezed.reshape(channels, BINS * BINS), preferred_element_type=jnp.float32)
            grid = grid + update.reshape(channels, BINS, BINS)
        final_act = jax.nn.relu(grid).astype(jnp.bfloat16)
        contact_maps = jnp.dot(head_weight, final_act.reshape(channels, BINS * BINS), preferred_element_type=jnp.float32)
        skewed = skew_square(contact_maps.reshape(TARGETS, BINS, BINS))
        return skewed * row_weight[None, :, None]

    weighted = lax.map(one_window, jnp.arange(N_GENOME, dtype=jnp.int32))
    blocks = BINS // STRIDE
    stacked_blocks = weighted.reshape(N_GENOME, TARGETS, blocks, STRIDE, BINS)
    numerator = jnp.zeros((N_GENOME, TARGETS, STRIDE, BINS), jnp.float32)
    weight_sum = jnp.zeros((N_GENOME, STRIDE, BINS), jnp.float32)
    owner = jnp.arange(N_GENOME)
    offsets = jnp.arange(BINS)
    local_rows = jnp.arange(STRIDE)
    for block_index in range(blocks):
        moved = jnp.pad(stacked_blocks[:, :, block_index], ((block_index, 0), (0, 0), (0, 0), (0, 0)))[:N_GENOME]
        numerator = numerator + moved
        window_rows = STRIDE * block_index + local_rows
        covered = (owner[:, None, None] >= block_index) & (window_rows[None, :, None] + offsets[None, None, :] < BINS)
        weight_sum = weight_sum + jnp.where(covered, row_weight[window_rows][None, :, None], 0.0)
    stitched = numerator / jnp.maximum(weight_sum, 1.0)[:, None]
    total_rows = N_GENOME * STRIDE
    stitched = jnp.transpose(stitched, (1, 0, 2, 3)).reshape(TARGETS, total_rows, BINS)

    extended = jnp.pad(stitched, ((0, 0), (STRIDE, 0), (0, 0)))
    prefix = jnp.concatenate([jnp.zeros((TARGETS, total_rows + STRIDE, 1), jnp.float32), jnp.cumsum(extended, axis=2)], axis=2)
    square = prefix[:, :, STRIDE + 1:2 * STRIDE + 1] - prefix[:, :, 1:STRIDE + 1]
    contact = jnp.exp(extended[:, :, 1:STRIDE + 1])
    insulation = jnp.zeros((TARGETS, total_rows), jnp.float32)
    upstream = jnp.zeros((TARGETS, total_rows), jnp.float32)
    for column in range(STRIDE):
        insulation = insulation + square[:, STRIDE - column:STRIDE - column + total_rows, column]
        upstream = upstream + contact[:, STRIDE - column - 1:STRIDE - column - 1 + total_rows, column]
    insulation = insulation / (STRIDE * STRIDE)
    downstream = jnp.sum(contact[:, STRIDE:], axis=2)
    direction = (downstream - upstream) / (downstream + upstream)
    return stitched, jnp.stack([insulation, direction])
```

```python
import functools

import jax
import jax.numpy as jnp
from jax import lax
from jax.experimental import pallas as pl
from jax.experimental.pallas import tpu as pltpu
from jax.sharding import PartitionSpec as P

BP = 2048
STRIDE = 64
BINS = 256
BLOCKS = 4
C1 = 96
MID = 48
C2 = 48
TARGETS = 5
TRUNK = 6
HEIGHT = 16
F32 = jnp.float32
BF16 = jnp.bfloat16
CHUNKS = 4


def iota(shape, dim):
    return lax.broadcasted_iota(jnp.int32, shape, dim)


def dot(a, b):
    return jnp.dot(a, b, preferred_element_type=F32)


def shifted(value, first, last):
    width = value.shape[1]
    lane = iota(value.shape, 1)
    zero = jnp.zeros_like(value)
    before = pltpu.roll(value, 1, 1)
    after = pltpu.roll(value, width - 1, 1)
    if first:
        before = jnp.where(lane == 0, zero, before)
    if last:
        after = jnp.where(lane == width - 1, zero, after)
    return before, after


def skewed(value, sign):
    width = value.shape[2]
    row = iota(value.shape, 1)
    for bit in (1, 2, 4, 8):
        turned = pltpu.roll(value, bit if sign > 0 else width - bit, 2)
        value = jnp.where(jnp.bitwise_and(row, bit) != 0, turned, value)
    return value


def kernel(
    genomes,
    towers,
    bases_hbm,
    stitch_hbm,
    stem_hbm,
    trunk_in_hbm,
    trunk_out_hbm,
    pair_hbm,
    rate_hbm,
    conv_hbm,
    mix_hbm,
    head_hbm,
    band_hbm,
    scores_hbm,
    bases,
    stitch,
    stem,
    trunk_in,
    trunk_out,
    pair,
    rate,
    conv,
    mix,
    head,
    onehot,
    window,
    taps,
    wide_conv,
    wide_mix,
    wide_head,
    decay,
    rates,
    row_weights,
    left,
    right,
    x1,
    x2,
    grid1,
    final,
    sent,
    landed,
    own_piece,
    band,
    part,
    parts_in,
    scores,
    in_sems,
    stem_sems,
    out_sems,
    feature_send,
    feature_recv,
    piece_send,
    piece_recv,
    part_send,
    part_recv,
):
    g = lax.axis_index("genome")
    t = lax.axis_index("tower")

    def at_genome(step):
        return {"genome": lax.rem(g + step + genomes, genomes), "tower": t}

    def at_band(step):
        place = t + step + towers
        up = lax.div(place, towers) - 1
        return {"genome": lax.rem(g + up + genomes, genomes), "tower": lax.rem(place, towers)}

    barrier = pltpu.get_barrier_semaphore()
    peers = [at_genome(s) for s in (-1, 1, -2, 2, -3, 3)] + [at_band(s) for s in (-1, 1, -2, 2, -3, 3)]
    for peer in peers:
        pl.semaphore_signal(barrier, inc=1, device_id=peer, device_id_type=pl.DeviceIdType.MESH)

    chunk = 4 * BP // CHUNKS
    bases_copy = pltpu.make_async_copy(bases_hbm, bases, in_sems.at[0])
    bases_copy.start()
    stem_copies = []
    for k in range(CHUNKS):
        lanes = pl.ds(k * chunk, chunk)
        stem_copies.append(pltpu.make_async_copy(stem_hbm.at[:, lanes], stem.at[:, lanes], stem_sems.at[k]))
        stem_copies[-1].start()
    small = [
        (stitch_hbm, stitch),
        (trunk_in_hbm, trunk_in),
        (trunk_out_hbm, trunk_out),
        (pair_hbm, pair),
        (rate_hbm, rate),
        (conv_hbm, conv),
        (mix_hbm, mix),
        (head_hbm, head),
    ]
    small_copies = [pltpu.make_async_copy(a, b, in_sems.at[i + 1]) for i, (a, b) in enumerate(small)]
    for copy in small_copies:
        copy.start()

    bases_copy.wait()
    spread = jnp.where(lax.shift_right_logical(iota((128, 512), 1), 2) == iota((128, 512), 0), 1.0, 0.0).astype(BF16)
    letter = jnp.bitwise_and(iota((STRIDE, 512), 1), 3).astype(F32)
    summed = jnp.zeros((STRIDE, C1), F32)
    for k in range(CHUNKS):
        for q in range(16 // CHUNKS):
            rows = bases[pl.ds(k * (16 // CHUNKS) + q, STRIDE, stride=16), :]
            repeated = dot(rows.astype(F32).astype(BF16), spread)
            onehot[:, pl.ds(q * 512, 512)] = jnp.where(repeated == letter, 1.0, 0.0).astype(BF16)
        stem_copies[k].wait()
        summed = summed + lax.dot_general(
            onehot[...], stem[:, pl.ds(k * chunk, chunk)], (((1,), (1,)), ((), ())), preferred_element_type=F32
        )
    window[0] = jnp.concatenate([summed, jnp.zeros((STRIDE, 128 - C1), F32)], axis=1).astype(BF16)

    pl.semaphore_wait(barrier, len(peers))
    feature_copies = []
    for s in range(1, BLOCKS):
        feature_copies.append(
            pltpu.make_async_remote_copy(
                src_ref=window.at[0],
                dst_ref=window.at[s],
                send_sem=feature_send.at[s - 1],
                recv_sem=feature_recv.at[s - 1],
                device_id=at_genome(-s),
                device_id_type=pl.DeviceIdType.MESH,
            )
        )
        feature_copies[-1].start()

    for copy in small_copies:
        copy.wait()
    for l in range(TRUNK):
        for q in range(3):
            taps[l, pl.ds(q * MID, MID), :] = trunk_in[l, :, pl.ds(q * C1, C1)]
    for l in range(2):
        for o in range(3):
            parts = []
            if o:
                parts.append(jnp.zeros((C2, 144 * o), BF16))
            parts += [conv[l, u] for u in range(3)]
            if o < 2:
                parts.append(jnp.zeros((C2, 144 * (2 - o)), BF16))
            wide_conv[l, pl.ds(o * C2, C2), :] = jnp.concatenate(parts, axis=1)
            parts = []
            if o:
                parts.append(jnp.zeros((C2, C2 * o), BF16))
            parts.append(mix[l])
            if o < 2:
                parts.append(jnp.zeros((C2, C2 * (2 - o)), BF16))
            wide_mix[l, pl.ds(o * C2, C2), :] = jnp.concatenate(parts, axis=1)
    lane = iota((C2, HEIGHT * C2), 1)
    row_of = lax.shift_right_logical(lane * 1366, 16)
    tile = jnp.where(lane - row_of * C2 == iota((C2, HEIGHT * C2), 0), 1.0, 0.0).astype(BF16)
    head_rows = jnp.concatenate(
        [jnp.broadcast_to(head[k : k + 1].astype(F32), (HEIGHT, C2)) for k in range(TARGETS)], axis=0
    ).astype(BF16)
    many = (TARGETS * HEIGHT, HEIGHT * C2)
    row_of = lax.shift_right_logical(iota(many, 1) * 1366, 16)
    wide_head[...] = jnp.where(
        row_of == jnp.bitwise_and(iota(many, 0), HEIGHT - 1), dot(head_rows, tile), 0.0
    ).astype(BF16)
    first_row = HEIGHT * t
    for b in range(BLOCKS):
        rows = STRIDE * b - 2 + first_row + iota((24, BINS), 0)
        gap = jnp.abs(rows - iota((24, BINS), 1)).astype(F32)
        decay[b] = jnp.log(1.0 + gap)
    square = (C2, C2)
    column = jnp.sum(
        jnp.where(iota(square, 0) == iota(square, 1), jnp.broadcast_to(rate[...], square), 0.0), axis=1, keepdims=True
    )
    rates[...] = jnp.broadcast_to(column, (C2, 128))
    band_shape = (HEIGHT, BINS)
    weights = jnp.broadcast_to(stitch[...].astype(F32), band_shape)
    lane = iota(band_shape, 1)
    row = iota(band_shape, 0)
    total = jnp.zeros(band_shape, F32)
    for b in range(BLOCKS):
        place = STRIDE * b + first_row + row
        column = jnp.sum(jnp.where(lane == place, weights, 0.0), axis=1, keepdims=True)
        column = jnp.broadcast_to(column, band_shape)
        inside = lane + place < BINS
        row_weights[b] = jnp.where(inside, column, 0.0)
        total = total + jnp.where(jnp.logical_and(inside, g >= b), column, 0.0)
    row_weights[BLOCKS] = 1.0 / jnp.maximum(total, 1.0)

    for copy in feature_copies:
        copy.wait_recv()
    slots = [window[0].astype(F32)]
    for s in range(1, BLOCKS):
        slots.append(jnp.where(g + s < genomes, window[s].astype(F32), 0.0))
    stream = jnp.concatenate(slots, axis=0).T[:C1]
    lane = iota((MID, BINS), 1)
    for l in range(TRUNK):
        dilation = max(1, BINS // 2 ** (TRUNK - l))
        taken = dot(taps[l], jnp.maximum(stream, 0.0).astype(BF16))
        before = jnp.where(lane >= dilation, pltpu.roll(taken[:MID], dilation, 1), 0.0)
        after = jnp.where(lane < BINS - dilation, pltpu.roll(taken[2 * MID :], BINS - dilation, 1), 0.0)
        squeezed = jnp.maximum(before + taken[MID : 2 * MID] + after, 0.0).astype(BF16)
        stream = stream + dot(trunk_out[l], squeezed)
    projected = dot(pair[...], jnp.maximum(stream, 0.0).astype(BF16))
    left[...] = pltpu.roll(projected[:C2], lax.rem(2 - first_row + BINS, BINS), 1)
    right[...] = projected[C2:]

    piece_copies = []
    for b in range(BLOCKS - 1, -1, -1):
        lo = 128 if b == 3 else 0
        width = BINS - lo
        lanes = pl.ds(lo, width)
        first = lo == 0

        def put(ref, at, value):
            before, after = shifted(value, first, True)
            ref[pl.ds(at, C2), lanes] = before
            ref[pl.ds(at + C2, C2), lanes] = value
            ref[pl.ds(at + 2 * C2, C2), lanes] = after

        base = STRIDE * b - 2 + first_row
        decline = jnp.concatenate([rates[...]] * (width // 128), axis=1)
        for r in range(HEIGHT + 4):
            at = STRIDE * b + r
            mixed = (
                jnp.broadcast_to(left[:, at : at + 1], (C2, width))
                + right[:, lanes]
                - decline * jnp.broadcast_to(decay[b, r : r + 1, lanes], (C2, width))
            )
            mixed = jnp.maximum(mixed, 0.0)
            if (b == 0 and r < 2) or (b == BLOCKS - 1 and r >= HEIGHT + 2):
                mixed = jnp.where(jnp.logical_and(base + r >= 0, base + r < BINS), mixed, 0.0)
            put(x1, 144 * r, mixed.astype(BF16))

        for k in range(6):
            convolved = dot(wide_conv[0], x1[pl.ds(432 * k, 720), lanes])
            mixed = dot(wide_mix[0], jnp.maximum(convolved, 0.0).astype(BF16))
            for o in range(3):
                r = 3 * k + o + 1
                held = x1[pl.ds(144 * r + C2, C2), lanes].astype(F32)
                value = held + mixed[o * C2 : (o + 1) * C2]
                grid1[pl.ds(C2 * (r - 1), C2), lanes] = value
                value = jnp.maximum(value, 0.0)
                if (b == 0 and r < 2) or (b == BLOCKS - 1 and r >= HEIGHT + 2):
                    value = jnp.where(jnp.logical_and(base + r >= 0, base + r < BINS), value, 0.0)
                put(x2, 144 * (r - 1), value.astype(BF16))

        for k in range(6):
            r0 = min(3 * k, HEIGHT - 3)
            convolved = dot(wide_conv[1], x2[pl.ds(144 * r0, 720), lanes])
            mixed = dot(wide_mix[1], jnp.maximum(convolved, 0.0).astype(BF16))
            value = grid1[pl.ds(C2 * (r0 + 1), 144), lanes] + mixed
            final[pl.ds(C2 * r0, 144), lanes] = jnp.maximum(value, 0.0).astype(BF16)

        contact = dot(wide_head[...], final[:, lanes])
        if lo:
            contact = jnp.concatenate([jnp.zeros((TARGETS * HEIGHT, lo), F32), contact], axis=1)
        contact = contact.reshape(TARGETS, HEIGHT, BINS)
        turn = lax.rem(2 * BINS - STRIDE * b - first_row, BINS)
        piece = skewed(pltpu.roll(contact, turn, 2), -1) * row_weights[b][None]
        if b == 0:
            own_piece[...] = piece
        else:
            span = BINS if b == 1 else 128
            sent[b - 1] = piece.astype(BF16)
            copy = pltpu.make_async_remote_copy(
                src_ref=sent.at[b - 1, :, :, pl.ds(0, span)],
                dst_ref=landed.at[b - 1, :, :, pl.ds(0, span)],
                send_sem=piece_send.at[b - 1],
                recv_sem=piece_recv.at[b - 1],
                device_id=at_genome(b),
                device_id_type=pl.DeviceIdType.MESH,
            )
            copy.start()
            piece_copies.append(copy)

    for copy in piece_copies:
        copy.wait_recv()
    near = own_piece[:, :, :128]
    for b in range(1, BLOCKS):
        near = near + jnp.where(g >= b, landed[b - 1, :, :, :128].astype(F32), 0.0)
    far = own_piece[:, :, 128:] + jnp.where(g >= 1, landed[0, :, :, 128:].astype(F32), 0.0)
    near = near * row_weights[BLOCKS, :, :128][None]
    band[:, :, :128] = near
    band[:, :, 128:] = far * row_weights[BLOCKS, :, 128:][None]
    band_copy = pltpu.make_async_copy(band, band_hbm, out_sems.at[0])
    band_copy.start()

    shape = (TARGETS, HEIGHT, 128)
    lane = iota(shape, 2)
    run = near
    for step in (1, 2, 4, 8, 16, 32):
        run = run + pltpu.roll(run, 128 - step, 2)
    inside = jnp.where(jnp.logical_and(lane >= 1, lane <= STRIDE), run, 0.0)
    insulation = jnp.sum(skewed(pltpu.roll(inside, 127, 2), 1), axis=1)
    contact = jnp.where(jnp.logical_and(lane >= 1, lane <= STRIDE), jnp.exp(near), 0.0)
    upstream = jnp.sum(skewed(contact, 1), axis=1)
    downstream = jnp.sum(contact, axis=2, keepdims=True)
    downstream = jnp.sum(jnp.where(lane == iota(shape, 1), jnp.broadcast_to(downstream, shape), 0.0), axis=1)
    part[0:TARGETS] = insulation
    part[8 : 8 + TARGETS] = upstream
    part_copies = []
    for m in range(1, BLOCKS + 1):
        copy = pltpu.make_async_remote_copy(
            src_ref=part,
            dst_ref=parts_in.at[m - 1],
            send_sem=part_send.at[m - 1],
            recv_sem=part_recv.at[m - 1],
            device_id=at_band(m),
            device_id_type=pl.DeviceIdType.MESH,
        )
        copy.start()
        part_copies.append(copy)
    for copy in part_copies:
        copy.wait_recv()
    place = g * towers + t
    flat = (TARGETS, 128)
    lane = iota(flat, 1)
    for m in range(1, BLOCKS + 1):
        turn = 128 - HEIGHT * m
        absent = float(HEIGHT) if m < BLOCKS else (HEIGHT - lane).astype(F32)
        insulation = insulation + jnp.where(place >= m, pltpu.roll(parts_in[m - 1, 0:TARGETS], turn, 1), 0.0)
        upstream = upstream + jnp.where(place >= m, pltpu.roll(parts_in[m - 1, 8 : 8 + TARGETS], turn, 1), absent)
    scores[0] = (insulation * (1.0 / (STRIDE * STRIDE)))[:, :HEIGHT]
    scores[1] = ((downstream - upstream) / (downstream + upstream))[:, :HEIGHT]
    scores_copy = pltpu.make_async_copy(scores, scores_hbm, out_sems.at[1])
    scores_copy.start()
    for copy in feature_copies + piece_copies + part_copies:
        copy.wait_send()
    band_copy.wait()
    scores_copy.wait()


def solution(mesh):
    genomes, towers = mesh.shape["genome"], mesh.shape["tower"]

    def per_device(bases, stitch, stem, trunk_in, trunk_out, pair, rate, conv, mix, head):
        anywhere = pl.BlockSpec(memory_space=pl.ANY)
        vmem = pltpu.VMEM
        dma = pltpu.SemaphoreType.DMA
        many = TARGETS * HEIGHT
        return pl.pallas_call(
            functools.partial(kernel, genomes, towers),
            out_shape=(
                jax.ShapeDtypeStruct((TARGETS, HEIGHT, BINS), F32),
                jax.ShapeDtypeStruct((2, TARGETS, HEIGHT), F32),
            ),
            in_specs=[anywhere] * 10,
            out_specs=(anywhere, anywhere),
            scratch_shapes=[
                vmem((1024, 128), jnp.int32),
                vmem((1, BINS), jnp.int32),
                vmem((C1, 4 * BP), BF16),
                vmem((TRUNK, MID, 3 * C1), BF16),
                vmem((TRUNK, C1, MID), BF16),
                vmem((2 * C2, C1), BF16),
                vmem((1, C2), F32),
                vmem((2, 3, C2, 3 * C2), BF16),
                vmem((2, C2, C2), BF16),
                vmem((TARGETS, C2), BF16),
                vmem((STRIDE, 4 * BP // CHUNKS), BF16),
                vmem((BLOCKS, STRIDE, 128), BF16),
                vmem((TRUNK, 3 * MID, C1), BF16),
                vmem((2, 3 * C2, 15 * C2), BF16),
                vmem((2, 3 * C2, 3 * C2), BF16),
                vmem((many, HEIGHT * C2), BF16),
                vmem((BLOCKS, 24, BINS), F32),
                vmem((C2, 128), F32),
                vmem((BLOCKS + 1, HEIGHT, BINS), F32),
                vmem((C2, BINS), F32),
                vmem((C2, BINS), F32),
                vmem((20 * 144, BINS), BF16),
                vmem((18 * 144, BINS), BF16),
                vmem((18 * C2, BINS), F32),
                vmem((HEIGHT * C2, BINS), BF16),
                vmem((BLOCKS - 1, TARGETS, HEIGHT, BINS), BF16),
                vmem((BLOCKS - 1, TARGETS, HEIGHT, BINS), BF16),
                vmem((TARGETS, HEIGHT, BINS), F32),
                vmem((TARGETS, HEIGHT, BINS), F32),
                vmem((16, 128), F32),
                vmem((BLOCKS, 16, 128), F32),
                vmem((2, TARGETS, HEIGHT), F32),
                dma((9,)),
                dma((CHUNKS,)),
                dma((2,)),
                dma((BLOCKS - 1,)),
                dma((BLOCKS - 1,)),
                dma((BLOCKS - 1,)),
                dma((BLOCKS - 1,)),
                dma((BLOCKS,)),
                dma((BLOCKS,)),
            ],
            compiler_params=pltpu.CompilerParams(collective_id=0, has_side_effects=True),
            name="contacts",
        )(
            bases.reshape(-1, 128),
            stitch.reshape(1, -1),
            stem,
            trunk_in,
            trunk_out,
            pair,
            rate.reshape(1, -1),
            conv,
            mix,
            head,
        )

    placed = (P("genome"), P(), P(), P(), P(), P(), P(), P(), P(), P())
    return jax.shard_map(
        per_device,
        mesh=mesh,
        in_specs=placed,
        out_specs=(P(None, ("genome", "tower"), None), P(None, None, ("genome", "tower"))),
        check_vma=False,
    )
```

```python
import functools

import jax
import jax.numpy as jnp
from jax import lax
from jax.experimental import pallas as pl
from jax.experimental.pallas import tpu as pltpu
from jax.sharding import PartitionSpec as P

BP = 2048
STRIDE = 64
BINS = 256
BLOCKS = 4
C1 = 96
MID = 48
C2 = 48
TARGETS = 5
TRUNK = 6
HEIGHT = 16
F32 = jnp.float32
BF16 = jnp.bfloat16
CHUNKS = 4


def iota(shape, dim):
    return lax.broadcasted_iota(jnp.int32, shape, dim)


def dot(a, b):
    return jnp.dot(a, b, preferred_element_type=F32)


def shifted(value, first, last):
    width = value.shape[1]
    lane = iota(value.shape, 1)
    zero = jnp.zeros_like(value)
    before = pltpu.roll(value, 1, 1)
    after = pltpu.roll(value, width - 1, 1)
    if first:
        before = jnp.where(lane == 0, zero, before)
    if last:
        after = jnp.where(lane == width - 1, zero, after)
    return before, after


def skewed(value, sign):
    width = value.shape[2]
    row = iota(value.shape, 1)
    for bit in (1, 2, 4, 8):
        turned = pltpu.roll(value, bit if sign > 0 else width - bit, 2)
        value = jnp.where(jnp.bitwise_and(row, bit) != 0, turned, value)
    return value


def kernel(
    genomes,
    towers,
    bases_hbm,
    stitch_hbm,
    stem_hbm,
    trunk_in_hbm,
    trunk_out_hbm,
    pair_hbm,
    rate_hbm,
    conv_hbm,
    mix_hbm,
    head_hbm,
    band,
    scores,
    bases,
    stitch,
    stem,
    trunk_in,
    trunk_out,
    pair,
    rate,
    conv,
    mix,
    head,
    onehot,
    window,
    taps,
    widen,
    wide_conv,
    wide_mix,
    wide_head,
    decay,
    rates,
    row_weights,
    left,
    right,
    x1,
    x2,
    grid1,
    final,
    sent,
    landed,
    own_piece,
    part,
    parts_in,
    in_sems,
    stem_sems,
    feature_send,
    feature_recv,
    piece_send,
    piece_recv,
    part_send,
    part_recv,
):
    g = lax.axis_index("genome")
    t = lax.axis_index("tower")

    place = g * towers + t

    def at_genome(step):
        return {"genome": g + step, "tower": t}, jnp.logical_and(g + step >= 0, g + step < genomes)

    def at_band(step):
        up = lax.div(t + step + towers, towers) - 1
        near = {"genome": g + up, "tower": t + step - up * towers}
        return near, jnp.logical_and(place + step >= 0, place + step < genomes * towers)

    barrier = pltpu.get_barrier_semaphore()
    steps = (-1, 1, -2, 2, -3, 3)
    present = jnp.int32(0)
    for device, there in [at_genome(s) for s in steps] + [at_band(s) for s in steps]:
        present = present + there.astype(jnp.int32)

        @pl.when(there)
        def _():
            pl.semaphore_signal(barrier, inc=1, device_id=device, device_id_type=pl.DeviceIdType.MESH)

    chunk = 4 * BP // CHUNKS
    bases_copy = pltpu.make_async_copy(bases_hbm, bases, in_sems.at[0])
    bases_copy.start()
    stem_copies = []
    for k in range(CHUNKS):
        lanes = pl.ds(k * chunk, chunk)
        stem_copies.append(pltpu.make_async_copy(stem_hbm.at[:, lanes], stem.at[:, lanes], stem_sems.at[k]))
        stem_copies[-1].start()
    small = [
        (stitch_hbm, stitch),
        (trunk_in_hbm, trunk_in),
        (trunk_out_hbm, trunk_out),
        (pair_hbm, pair),
        (rate_hbm, rate),
        (conv_hbm, conv),
        (mix_hbm, mix),
        (head_hbm, head),
    ]
    small_copies = [pltpu.make_async_copy(a, b, in_sems.at[i + 1]) for i, (a, b) in enumerate(small)]
    for copy in small_copies:
        copy.start()

    bases_copy.wait()
    spread = jnp.where(lax.shift_right_logical(iota((128, 512), 1), 2) == iota((128, 512), 0), 1.0, 0.0).astype(BF16)
    letter = jnp.bitwise_and(iota((STRIDE, 512), 1), 3).astype(F32)
    summed = jnp.zeros((STRIDE, C1), F32)
    for k in range(CHUNKS):
        for q in range(16 // CHUNKS):
            rows = bases[pl.ds(k * (16 // CHUNKS) + q, STRIDE, stride=16), :]
            repeated = dot(rows.astype(F32).astype(BF16), spread)
            onehot[:, pl.ds(q * 512, 512)] = jnp.where(repeated == letter, 1.0, 0.0).astype(BF16)
        stem_copies[k].wait()
        summed = summed + lax.dot_general(
            onehot[...], stem[:, pl.ds(k * chunk, chunk)], (((1,), (1,)), ((), ())), preferred_element_type=F32
        )
    window[0] = jnp.concatenate([summed, jnp.zeros((STRIDE, 128 - C1), F32)], axis=1).astype(BF16)

    pl.semaphore_wait(barrier, present)
    sends = []

    def send(source, target, send_sem, recv_sem, to):
        device, there = to
        copy = pltpu.make_async_remote_copy(
            src_ref=source,
            dst_ref=target,
            send_sem=send_sem,
            recv_sem=recv_sem,
            device_id=device,
            device_id_type=pl.DeviceIdType.MESH,
        )

        @pl.when(there)
        def _():
            copy.start()

        sends.append((copy, there))
        return copy

    def receive(copy, there):
        @pl.when(there)
        def _():
            copy.wait_recv()

    feature_copies = []
    for s in range(1, BLOCKS):
        feature_copies.append(
            send(window.at[0], window.at[s], feature_send.at[s - 1], feature_recv.at[s - 1], at_genome(-s))
        )

    for copy in small_copies:
        copy.wait()
    for l in range(TRUNK):
        for q in range(3):
            taps[l, pl.ds(q * MID, MID), :] = trunk_in[l, :, pl.ds(q * C1, C1)]
        widen[l] = trunk_out[l].astype(F32).T.astype(BF16)
    for l in range(2):
        for o in range(3):
            parts = []
            if o:
                parts.append(jnp.zeros((C2, 144 * o), BF16))
            parts += [conv[l, u] for u in range(3)]
            if o < 2:
                parts.append(jnp.zeros((C2, 144 * (2 - o)), BF16))
            wide_conv[l, pl.ds(o * C2, C2), :] = jnp.concatenate(parts, axis=1)
            parts = []
            if o:
                parts.append(jnp.zeros((C2, C2 * o), BF16))
            parts.append(mix[l])
            if o < 2:
                parts.append(jnp.zeros((C2, C2 * (2 - o)), BF16))
            wide_mix[l, pl.ds(o * C2, C2), :] = jnp.concatenate(parts, axis=1)
    lane = iota((C2, HEIGHT * C2), 1)
    row_of = lax.shift_right_logical(lane * 1366, 16)
    tile = jnp.where(lane - row_of * C2 == iota((C2, HEIGHT * C2), 0), 1.0, 0.0).astype(BF16)
    head_rows = jnp.concatenate(
        [jnp.broadcast_to(head[k : k + 1].astype(F32), (HEIGHT, C2)) for k in range(TARGETS)], axis=0
    ).astype(BF16)
    many = (TARGETS * HEIGHT, HEIGHT * C2)
    row_of = lax.shift_right_logical(iota(many, 1) * 1366, 16)
    wide_head[...] = jnp.where(
        row_of == jnp.bitwise_and(iota(many, 0), HEIGHT - 1), dot(head_rows, tile), 0.0
    ).astype(BF16)
    first_row = HEIGHT * t
    for b in range(BLOCKS):
        rows = STRIDE * b - 2 + first_row + iota((24, BINS), 0)
        gap = jnp.abs(rows - iota((24, BINS), 1)).astype(F32)
        decay[b] = jnp.log(1.0 + gap)
    square = (C2, C2)
    column = jnp.sum(
        jnp.where(iota(square, 0) == iota(square, 1), jnp.broadcast_to(rate[...], square), 0.0), axis=1, keepdims=True
    )
    rates[...] = jnp.broadcast_to(column, (C2, 128))
    band_shape = (HEIGHT, BINS)
    weights = jnp.broadcast_to(stitch[...].astype(F32), band_shape)
    lane = iota(band_shape, 1)
    row = iota(band_shape, 0)
    total = jnp.zeros(band_shape, F32)
    for b in range(BLOCKS):
        spot = STRIDE * b + first_row + row
        column = jnp.sum(jnp.where(lane == spot, weights, 0.0), axis=1, keepdims=True)
        column = jnp.broadcast_to(column, band_shape)
        inside = lane + spot < BINS
        row_weights[b] = jnp.where(inside, column, 0.0)
        total = total + jnp.where(jnp.logical_and(inside, g >= b), column, 0.0)
    row_weights[BLOCKS] = 1.0 / jnp.maximum(total, 1.0)

    for s, copy in enumerate(feature_copies):
        receive(copy, g + s + 1 < genomes)
    slots = [window[0].astype(F32)]
    for s in range(1, BLOCKS):
        slots.append(jnp.where(g + s < genomes, window[s].astype(F32), 0.0))
    stream = jnp.concatenate(slots, axis=0).T[:C1]
    lane = iota((MID, BINS), 1)
    for l in range(TRUNK):
        dilation = max(1, BINS // 2 ** (TRUNK - l))
        taken = dot(taps[l], jnp.maximum(stream, 0.0).astype(BF16))
        before = jnp.where(lane >= dilation, pltpu.roll(taken[:MID], dilation, 1), 0.0)
        after = jnp.where(lane < BINS - dilation, pltpu.roll(taken[2 * MID :], BINS - dilation, 1), 0.0)
        squeezed = jnp.maximum(before + taken[MID : 2 * MID] + after, 0.0).astype(BF16)
        stream = stream + dot(widen[l], squeezed)
    projected = dot(pair[...], jnp.maximum(stream, 0.0).astype(BF16))
    left[...] = pltpu.roll(projected[:C2], lax.rem(2 - first_row + BINS, BINS), 1)
    right[...] = projected[C2:]

    piece_copies = {}
    for b in range(BLOCKS - 1, -1, -1):
        lo = 128 if b == 3 else 0
        width = BINS - lo
        lanes = pl.ds(lo, width)
        first = lo == 0

        def put(ref, at, value):
            before, after = shifted(value, first, True)
            ref[pl.ds(at, C2), lanes] = before
            ref[pl.ds(at + C2, C2), lanes] = value
            ref[pl.ds(at + 2 * C2, C2), lanes] = after

        base = STRIDE * b - 2 + first_row
        decline = jnp.concatenate([rates[...]] * (width // 128), axis=1)
        for r in range(HEIGHT + 4):
            at = STRIDE * b + r
            mixed = (
                jnp.broadcast_to(left[:, at : at + 1], (C2, width))
                + right[:, lanes]
                - decline * jnp.broadcast_to(decay[b, r : r + 1, lanes], (C2, width))
            )
            mixed = jnp.maximum(mixed, 0.0)
            if (b == 0 and r < 2) or (b == BLOCKS - 1 and r >= HEIGHT + 2):
                mixed = jnp.where(jnp.logical_and(base + r >= 0, base + r < BINS), mixed, 0.0)
            put(x1, 144 * r, mixed.astype(BF16))

        for k in range(6):
            convolved = dot(wide_conv[0], x1[pl.ds(432 * k, 720), lanes])
            mixed = dot(wide_mix[0], jnp.maximum(convolved, 0.0).astype(BF16))
            for o in range(3):
                r = 3 * k + o + 1
                held = x1[pl.ds(144 * r + C2, C2), lanes].astype(F32)
                value = held + mixed[o * C2 : (o + 1) * C2]
                grid1[pl.ds(C2 * (r - 1), C2), lanes] = value
                value = jnp.maximum(value, 0.0)
                if (b == 0 and r < 2) or (b == BLOCKS - 1 and r >= HEIGHT + 2):
                    value = jnp.where(jnp.logical_and(base + r >= 0, base + r < BINS), value, 0.0)
                put(x2, 144 * (r - 1), value.astype(BF16))

        for k in range(6):
            r0 = min(3 * k, HEIGHT - 3)
            convolved = dot(wide_conv[1], x2[pl.ds(144 * r0, 720), lanes])
            mixed = dot(wide_mix[1], jnp.maximum(convolved, 0.0).astype(BF16))
            value = grid1[pl.ds(C2 * (r0 + 1), 144), lanes] + mixed
            final[pl.ds(C2 * r0, 144), lanes] = jnp.maximum(value, 0.0).astype(BF16)

        contact = dot(wide_head[...], final[:, lanes])
        if lo:
            contact = jnp.concatenate([jnp.zeros((TARGETS * HEIGHT, lo), F32), contact], axis=1)
        contact = contact.reshape(TARGETS, HEIGHT, BINS)
        turn = lax.rem(2 * BINS - STRIDE * b - first_row, BINS)
        piece = skewed(pltpu.roll(contact, turn, 2), -1) * row_weights[b][None]
        if b == 0:
            own_piece[...] = piece
        else:
            span = BINS if b == 1 else 128
            sent[b - 1] = piece.astype(BF16)
            source, target = (ref.at[b - 1, :, :, pl.ds(0, span)] for ref in (sent, landed))
            piece_copies[b] = send(source, target, piece_send.at[b - 1], piece_recv.at[b - 1], at_genome(b))

    for b, copy in piece_copies.items():
        receive(copy, g >= b)
    near = own_piece[:, :, :128]
    for b in range(1, BLOCKS):
        near = near + jnp.where(g >= b, landed[b - 1, :, :, :128].astype(F32), 0.0)
    far = own_piece[:, :, 128:] + jnp.where(g >= 1, landed[0, :, :, 128:].astype(F32), 0.0)
    near = near * row_weights[BLOCKS, :, :128][None]
    band[:, :, :128] = near
    band[:, :, 128:] = far * row_weights[BLOCKS, :, 128:][None]

    shape = (TARGETS, HEIGHT, 128)
    lane = iota(shape, 2)
    run = near
    for step in (1, 2, 4, 8, 16, 32):
        run = run + pltpu.roll(run, 128 - step, 2)
    inside = jnp.where(jnp.logical_and(lane >= 1, lane <= STRIDE), run, 0.0)
    insulation = jnp.sum(skewed(pltpu.roll(inside, 127, 2), 1), axis=1)
    contact = jnp.where(jnp.logical_and(lane >= 1, lane <= STRIDE), jnp.exp(near), 0.0)
    upstream = jnp.sum(skewed(contact, 1), axis=1)
    downstream = jnp.sum(contact, axis=2, keepdims=True)
    downstream = jnp.sum(jnp.where(lane == iota(shape, 1), jnp.broadcast_to(downstream, shape), 0.0), axis=1)
    part[0:TARGETS] = insulation
    part[8 : 8 + TARGETS] = upstream
    part_copies = [
        send(part, parts_in.at[m - 1], part_send.at[m - 1], part_recv.at[m - 1], at_band(m)) for m in range(1, BLOCKS + 1)
    ]
    for m, copy in enumerate(part_copies):
        receive(copy, place > m)
    flat = (TARGETS, 128)
    lane = iota(flat, 1)
    for m in range(1, BLOCKS + 1):
        turn = 128 - HEIGHT * m
        absent = float(HEIGHT) if m < BLOCKS else (HEIGHT - lane).astype(F32)
        insulation = insulation + jnp.where(place >= m, pltpu.roll(parts_in[m - 1, 0:TARGETS], turn, 1), 0.0)
        upstream = upstream + jnp.where(place >= m, pltpu.roll(parts_in[m - 1, 8 : 8 + TARGETS], turn, 1), absent)
    scores[:, 0, :] = (insulation * (1.0 / (STRIDE * STRIDE)))[:, :HEIGHT]
    scores[:, 1, :] = ((downstream - upstream) / (downstream + upstream))[:, :HEIGHT]
    for copy, there in sends:

        @pl.when(there)
        def _():
            copy.wait_send()


def hand_over(band, scores, band_hbm, scores_hbm, sems):
    copies = [pltpu.make_async_copy(a, b, sems.at[i]) for i, (a, b) in enumerate(((band, band_hbm), (scores, scores_hbm)))]
    for copy in copies:
        copy.start()
    for copy in copies:
        copy.wait()


def solution(mesh):
    genomes, towers = mesh.shape["genome"], mesh.shape["tower"]

    def per_device(bases, stitch, stem, trunk_in, trunk_out, pair, rate, conv, mix, head):
        anywhere = pl.BlockSpec(memory_space=pl.ANY)
        vmem = pltpu.VMEM
        dma = pltpu.SemaphoreType.DMA
        many = TARGETS * HEIGHT
        shapes = (
            jax.ShapeDtypeStruct((TARGETS, HEIGHT, BINS), F32),
            jax.ShapeDtypeStruct((TARGETS, 2, HEIGHT), F32),
        )
        in_vmem = pl.BlockSpec(memory_space=pltpu.VMEM)
        results = pl.pallas_call(
            functools.partial(kernel, genomes, towers),
            out_shape=shapes,
            in_specs=[anywhere] * 10,
            out_specs=(in_vmem, in_vmem),
            scratch_shapes=[
                vmem((1024, 128), jnp.int32),
                vmem((1, BINS), jnp.int32),
                vmem((C1, 4 * BP), BF16),
                vmem((TRUNK, MID, 3 * C1), BF16),
                vmem((TRUNK, MID, C1), BF16),
                vmem((2 * C2, C1), BF16),
                vmem((1, C2), F32),
                vmem((2, 3, C2, 3 * C2), BF16),
                vmem((2, C2, C2), BF16),
                vmem((TARGETS, C2), BF16),
                vmem((STRIDE, 4 * BP // CHUNKS), BF16),
                vmem((BLOCKS, STRIDE, 128), BF16),
                vmem((TRUNK, 3 * MID, C1), BF16),
                vmem((TRUNK, C1, MID), BF16),
                vmem((2, 3 * C2, 15 * C2), BF16),
                vmem((2, 3 * C2, 3 * C2), BF16),
                vmem((many, HEIGHT * C2), BF16),
                vmem((BLOCKS, 24, BINS), F32),
                vmem((C2, 128), F32),
                vmem((BLOCKS + 1, HEIGHT, BINS), F32),
                vmem((C2, BINS), F32),
                vmem((C2, BINS), F32),
                vmem((20 * 144, BINS), BF16),
                vmem((18 * 144, BINS), BF16),
                vmem((18 * C2, BINS), F32),
                vmem((HEIGHT * C2, BINS), BF16),
                vmem((BLOCKS - 1, TARGETS, HEIGHT, BINS), BF16),
                vmem((BLOCKS - 1, TARGETS, HEIGHT, BINS), BF16),
                vmem((TARGETS, HEIGHT, BINS), F32),
                vmem((16, 128), F32),
                vmem((BLOCKS, 16, 128), F32),
                dma((9,)),
                dma((CHUNKS,)),
                dma((BLOCKS - 1,)),
                dma((BLOCKS - 1,)),
                dma((BLOCKS - 1,)),
                dma((BLOCKS - 1,)),
                dma((BLOCKS,)),
                dma((BLOCKS,)),
            ],
            compiler_params=pltpu.CompilerParams(collective_id=0, has_side_effects=True),
            name="contacts",
        )(
            bases.reshape(-1, 128),
            stitch.reshape(1, -1),
            stem,
            trunk_in,
            jnp.swapaxes(trunk_out, 1, 2),
            pair,
            rate.reshape(1, -1),
            conv,
            mix,
            head,
        )
        band, scores = pl.pallas_call(
            hand_over,
            out_shape=shapes,
            in_specs=[in_vmem, in_vmem],
            out_specs=(anywhere, anywhere),
            scratch_shapes=[dma((2,))],
            name="hand_over",
        )(*results)
        return band, jnp.swapaxes(scores, 0, 1)

    placed = (P("genome"), P(), P(), P(), P(), P(), P(), P(), P(), P())
    return jax.shard_map(
        per_device,
        mesh=mesh,
        in_specs=placed,
        out_specs=(P(None, ("genome", "tower"), None), P(None, None, ("genome", "tower"))),
        check_vma=False,
    )
```

```python
import functools

import jax
import jax.numpy as jnp
from jax import lax
from jax.experimental import pallas as pl
from jax.experimental.pallas import tpu as pltpu
from jax.sharding import PartitionSpec as P

BP = 2048
STRIDE = 64
BINS = 256
BLOCKS = 4
C1 = 96
MID = 48
C2 = 48
TARGETS = 5
TRUNK = 6
HEIGHT = 16
F32 = jnp.float32
BF16 = jnp.bfloat16
CHUNKS = 4
SPLIT = 124
MOVED = 136


def iota(shape, dim):
    return lax.broadcasted_iota(jnp.int32, shape, dim)


def dot(a, b):
    return jnp.dot(a, b, preferred_element_type=F32)


def shifted(value, starts, ends):
    width = value.shape[1]
    lane = iota(value.shape, 1)
    zero = jnp.zeros_like(value)
    before = pltpu.roll(value, 1, 1)
    after = pltpu.roll(value, width - 1, 1)
    for place in starts:
        before = jnp.where(lane == place, zero, before)
    for place in ends:
        after = jnp.where(lane == place, zero, after)
    return before, after


def skewed(value, sign):
    width = value.shape[2]
    row = iota(value.shape, 1)
    for bit in (1, 2, 4, 8):
        turned = pltpu.roll(value, bit if sign > 0 else width - bit, 2)
        value = jnp.where(jnp.bitwise_and(row, bit) != 0, turned, value)
    return value


def kernel(
    genomes,
    towers,
    bases_hbm,
    stitch_hbm,
    stem_hbm,
    trunk_in_hbm,
    trunk_out_hbm,
    pair_hbm,
    rate_hbm,
    conv_hbm,
    mix_hbm,
    head_hbm,
    band,
    scores,
    bases,
    stitch,
    stem,
    trunk_in,
    trunk_out,
    pair,
    rate,
    conv,
    mix,
    head,
    onehot,
    window,
    taps,
    widen,
    wide_conv,
    wide_mix,
    wide_head,
    decay,
    rates,
    row_weights,
    left,
    right,
    x1,
    x2,
    grid1,
    final,
    sent,
    landed,
    own_piece,
    part,
    parts_in,
    in_sems,
    stem_sems,
    feature_send,
    feature_recv,
    piece_send,
    piece_recv,
    part_send,
    part_recv,
):
    g = lax.axis_index("genome")
    t = lax.axis_index("tower")

    place = g * towers + t

    def at_genome(step):
        return {"genome": g + step, "tower": t}, jnp.logical_and(g + step >= 0, g + step < genomes)

    def at_band(step):
        up = lax.div(t + step + towers, towers) - 1
        near = {"genome": g + up, "tower": t + step - up * towers}
        return near, jnp.logical_and(place + step >= 0, place + step < genomes * towers)

    barrier = pltpu.get_barrier_semaphore()
    steps = (-1, 1, -2, 2, -3, 3)
    present = jnp.int32(0)
    for device, there in [at_genome(s) for s in steps] + [at_band(s) for s in steps]:
        present = present + there.astype(jnp.int32)

        @pl.when(there)
        def _():
            pl.semaphore_signal(barrier, inc=1, device_id=device, device_id_type=pl.DeviceIdType.MESH)

    chunk = 4 * BP // CHUNKS
    bases_copy = pltpu.make_async_copy(bases_hbm, bases, in_sems.at[0])
    bases_copy.start()
    stem_copies = []
    for k in range(CHUNKS):
        lanes = pl.ds(k * chunk, chunk)
        stem_copies.append(pltpu.make_async_copy(stem_hbm.at[:, lanes], stem.at[:, lanes], stem_sems.at[k]))
        stem_copies[-1].start()
    small = [
        (stitch_hbm, stitch),
        (trunk_in_hbm, trunk_in),
        (trunk_out_hbm, trunk_out),
        (pair_hbm, pair),
        (rate_hbm, rate),
        (conv_hbm, conv),
        (mix_hbm, mix),
        (head_hbm, head),
    ]
    small_copies = [pltpu.make_async_copy(a, b, in_sems.at[i + 1]) for i, (a, b) in enumerate(small)]
    for copy in small_copies:
        copy.start()

    bases_copy.wait()
    spread = jnp.where(lax.shift_right_logical(iota((128, 512), 1), 2) == iota((128, 512), 0), 1.0, 0.0).astype(BF16)
    letter = jnp.bitwise_and(iota((STRIDE, 512), 1), 3).astype(F32)
    summed = jnp.zeros((STRIDE, C1), F32)
    for k in range(CHUNKS):
        for q in range(16 // CHUNKS):
            rows = bases[pl.ds(k * (16 // CHUNKS) + q, STRIDE, stride=16), :]
            repeated = dot(rows.astype(F32).astype(BF16), spread)
            onehot[:, pl.ds(q * 512, 512)] = jnp.where(repeated == letter, 1.0, 0.0).astype(BF16)
        stem_copies[k].wait()
        summed = summed + lax.dot_general(
            onehot[...], stem[:, pl.ds(k * chunk, chunk)], (((1,), (1,)), ((), ())), preferred_element_type=F32
        )
    window[0] = jnp.concatenate([summed, jnp.zeros((STRIDE, 128 - C1), F32)], axis=1).astype(BF16)

    pl.semaphore_wait(barrier, present)
    sends = []

    def send(source, target, send_sem, recv_sem, to):
        device, there = to
        copy = pltpu.make_async_remote_copy(
            src_ref=source,
            dst_ref=target,
            send_sem=send_sem,
            recv_sem=recv_sem,
            device_id=device,
            device_id_type=pl.DeviceIdType.MESH,
        )

        @pl.when(there)
        def _():
            copy.start()

        sends.append((copy, there))
        return copy

    def receive(copy, there):
        @pl.when(there)
        def _():
            copy.wait_recv()

    feature_copies = []
    for s in range(1, BLOCKS):
        feature_copies.append(
            send(window.at[0], window.at[s], feature_send.at[s - 1], feature_recv.at[s - 1], at_genome(-s))
        )

    for copy in small_copies:
        copy.wait()
    for l in range(TRUNK):
        for q in range(3):
            taps[l, pl.ds(q * MID, MID), :] = trunk_in[l, :, pl.ds(q * C1, C1)]
        widen[l] = trunk_out[l].astype(F32).T.astype(BF16)
    for l in range(2):
        for o in range(3):
            parts = []
            if o:
                parts.append(jnp.zeros((C2, 144 * o), BF16))
            parts += [conv[l, u] for u in range(3)]
            if o < 2:
                parts.append(jnp.zeros((C2, 144 * (2 - o)), BF16))
            wide_conv[l, pl.ds(o * C2, C2), :] = jnp.concatenate(parts, axis=1)
            parts = []
            if o:
                parts.append(jnp.zeros((C2, C2 * o), BF16))
            parts.append(mix[l])
            if o < 2:
                parts.append(jnp.zeros((C2, C2 * (2 - o)), BF16))
            wide_mix[l, pl.ds(o * C2, C2), :] = jnp.concatenate(parts, axis=1)
    lane = iota((C2, HEIGHT * C2), 1)
    row_of = lax.shift_right_logical(lane * 1366, 16)
    tile = jnp.where(lane - row_of * C2 == iota((C2, HEIGHT * C2), 0), 1.0, 0.0).astype(BF16)
    head_rows = jnp.concatenate(
        [jnp.broadcast_to(head[k : k + 1].astype(F32), (HEIGHT, C2)) for k in range(TARGETS)], axis=0
    ).astype(BF16)
    many = (TARGETS * HEIGHT, HEIGHT * C2)
    row_of = lax.shift_right_logical(iota(many, 1) * 1366, 16)
    wide_head[...] = jnp.where(
        row_of == jnp.bitwise_and(iota(many, 0), HEIGHT - 1), dot(head_rows, tile), 0.0
    ).astype(BF16)
    first_row = HEIGHT * t
    table = (24, BINS)
    lane = iota(table, 1)
    for tile in range(3):
        spot, col = STRIDE * tile, lane
        if tile == 2:
            spot, col = jnp.where(lane < SPLIT, 3 * STRIDE, 2 * STRIDE), jnp.where(lane < SPLIT, lane + MOVED, lane)
        rows = spot + first_row - 2 + iota(table, 0)
        gap = jnp.abs(rows - col).astype(F32)
        decay[tile] = jnp.where(jnp.logical_and(rows >= 0, rows < BINS), jnp.log(1.0 + gap), 1e30)
    square = (C2, C2)
    column = jnp.sum(
        jnp.where(iota(square, 0) == iota(square, 1), jnp.broadcast_to(rate[...], square), 0.0), axis=1, keepdims=True
    )
    rates[...] = jnp.broadcast_to(column, (C2, 128))
    band_shape = (HEIGHT, BINS)
    weights = jnp.broadcast_to(stitch[...].astype(F32), band_shape)
    lane = iota(band_shape, 1)
    row = iota(band_shape, 0)
    total = jnp.zeros(band_shape, F32)
    for b in range(BLOCKS):
        spot = STRIDE * b + first_row + row
        column = jnp.sum(jnp.where(lane == spot, weights, 0.0), axis=1, keepdims=True)
        column = jnp.broadcast_to(column, band_shape)
        inside = lane + spot < BINS
        row_weights[b] = jnp.where(inside, column, 0.0)
        total = total + jnp.where(jnp.logical_and(inside, g >= b), column, 0.0)
    row_weights[BLOCKS] = 1.0 / jnp.maximum(total, 1.0)

    for s, copy in enumerate(feature_copies):
        receive(copy, g + s + 1 < genomes)
    slots = [window[0].astype(F32)]
    for s in range(1, BLOCKS):
        slots.append(jnp.where(g + s < genomes, window[s].astype(F32), 0.0))
    stream = jnp.concatenate(slots, axis=0).T[:C1]
    lane = iota((MID, BINS), 1)
    for l in range(TRUNK):
        dilation = max(1, BINS // 2 ** (TRUNK - l))
        taken = dot(taps[l], jnp.maximum(stream, 0.0).astype(BF16))
        before = jnp.where(lane >= dilation, pltpu.roll(taken[:MID], dilation, 1), 0.0)
        after = jnp.where(lane < BINS - dilation, pltpu.roll(taken[2 * MID :], BINS - dilation, 1), 0.0)
        squeezed = jnp.maximum(before + taken[MID : 2 * MID] + after, 0.0).astype(BF16)
        stream = stream + dot(widen[l], squeezed)
    projected = dot(pair[...], jnp.maximum(stream, 0.0).astype(BF16))
    left[...] = pltpu.roll(projected[:C2], lax.rem(2 - first_row + BINS, BINS), 1)
    side = projected[C2:]
    right[0] = side
    right[1] = jnp.where(iota((C2, BINS), 1) < SPLIT, pltpu.roll(side, BINS - MOVED, 1), side)

    narrow = iota((C2, 128), 1) < SPLIT
    low = iota((C2, BINS), 1) < SPLIT

    def put(ref, at, value, tile):
        before, after = shifted(value, (0,) if tile == 0 else (), (BINS - 1, BINS - 1 - MOVED) if tile == 2 else (BINS - 1,))
        lanes = pl.ds(BINS * tile, BINS)
        ref[pl.ds(at, C2), lanes] = before
        ref[pl.ds(at + C2, C2), lanes] = value
        ref[pl.ds(at + 2 * C2, C2), lanes] = after

    def spread_column(at):
        return jnp.broadcast_to(left[:, at : at + 1], (C2, 128))

    def pair_row(r, tile):
        here = spread_column(STRIDE * tile + r)
        there = jnp.where(narrow, spread_column(3 * STRIDE + r), here) if tile == 2 else here
        decline = rates[...]
        halves = []
        for h, column in enumerate((there, here)):
            lanes = slice(128 * h, 128 * h + 128)
            fall = decline * jnp.broadcast_to(decay[tile, r : r + 1, lanes], (C2, 128))
            halves.append(jnp.maximum(column + right[tile // 2, :, lanes] - fall, 0.0))
        put(x1, 144 * r, jnp.concatenate(halves, axis=1).astype(BF16), tile)

    def convolve(l, ref, at, rows, tile):
        depth = 144 * (rows + 2)
        return dot(wide_conv[l, : C2 * rows, :depth], ref[pl.ds(144 * at, depth), pl.ds(BINS * tile, BINS)])

    def remix(l, convolved):
        rows = convolved.shape[0]
        return dot(wide_mix[l, :rows, :rows], jnp.maximum(convolved, 0.0).astype(BF16))

    def first_block(at, mixed, tile):
        for o in range(3):
            r = at + o + 1
            held = x1[pl.ds(144 * r + C2, C2), pl.ds(BINS * tile, BINS)].astype(F32)
            value = held + mixed[o * C2 : (o + 1) * C2]
            grid1[pl.ds(C2 * (r - 1), C2), pl.ds(BINS * tile, BINS)] = value
            value = jnp.maximum(value, 0.0)
            if tile == 0 and r == 1:
                value = jnp.where(t == 0, 0.0, value)
            if tile == 2 and r == HEIGHT + 2:
                value = jnp.where(jnp.logical_and(low, t == towers - 1), 0.0, value)
            put(x2, 144 * (r - 1), value.astype(BF16), tile)

    def second_block(at, mixed, tile):
        rows, lanes = mixed.shape[0], pl.ds(BINS * tile, BINS)
        value = grid1[pl.ds(C2 * (at + 1), rows), lanes] + mixed
        final[pl.ds(C2 * at, rows), lanes] = jnp.maximum(value, 0.0).astype(BF16)

    groups = ((0, 3), (3, 3), (6, 3), (9, 3), (12, 2), (14, 2))

    def tower(tiles):
        for r in range(5):
            for tile in tiles:
                pair_row(r, tile)
        for step in range(8):
            ones, twos = [], []
            if step < 6:
                ones = [convolve(0, x1, 3 * step, 3, tile) for tile in tiles]
            if step >= 2:
                at, rows = groups[step - 2]
                twos = [convolve(1, x2, at, rows, tile) for tile in tiles]
            for r in range(3 * step + 5, min(3 * step + 8, HEIGHT + 4)):
                for tile in tiles:
                    pair_row(r, tile)
            ones = [remix(0, value) for value in ones]
            twos = [remix(1, value) for value in twos]
            for tile, value in zip(tiles, ones):
                first_block(3 * step, value, tile)
            if twos:
                for tile, value in zip(tiles, twos):
                    second_block(at, value, tile)

    piece_copies = {}

    def piece_of(b, contact):
        start = STRIDE * b + first_row - (MOVED if b == 3 else 0)
        return skewed(pltpu.roll(contact, lax.rem(2 * BINS - start, BINS), 2), -1) * row_weights[b][None]

    def hand_on(b, piece):
        span = BINS if b == 1 else 128
        sent[b - 1] = piece.astype(BF16)
        source, target = (ref.at[b - 1, :, :, pl.ds(0, span)] for ref in (sent, landed))
        piece_copies[b] = send(source, target, piece_send.at[b - 1], piece_recv.at[b - 1], at_genome(b))

    def contact_of(tile):
        return dot(wide_head[...], final[:, pl.ds(BINS * tile, BINS)]).reshape(TARGETS, HEIGHT, BINS)

    tower((1, 2))
    contact = contact_of(2)
    hand_on(3, piece_of(3, contact))
    hand_on(2, piece_of(2, contact))
    hand_on(1, piece_of(1, contact_of(1)))
    tower((0,))
    own_piece[...] = piece_of(0, contact_of(0))

    for b, copy in piece_copies.items():
        receive(copy, g >= b)
    near = own_piece[:, :, :128]
    for b in range(1, BLOCKS):
        near = near + jnp.where(g >= b, landed[b - 1, :, :, :128].astype(F32), 0.0)
    far = own_piece[:, :, 128:] + jnp.where(g >= 1, landed[0, :, :, 128:].astype(F32), 0.0)
    near = near * row_weights[BLOCKS, :, :128][None]
    band[:, :, :128] = near
    band[:, :, 128:] = far * row_weights[BLOCKS, :, 128:][None]

    shape = (TARGETS, HEIGHT, 128)
    lane = iota(shape, 2)
    run = near
    for step in (1, 2, 4, 8, 16, 32):
        run = run + pltpu.roll(run, 128 - step, 2)
    inside = jnp.where(jnp.logical_and(lane >= 1, lane <= STRIDE), run, 0.0)
    insulation = jnp.sum(skewed(pltpu.roll(inside, 127, 2), 1), axis=1)
    contact = jnp.where(jnp.logical_and(lane >= 1, lane <= STRIDE), jnp.exp(near), 0.0)
    upstream = jnp.sum(skewed(contact, 1), axis=1)
    downstream = jnp.sum(contact, axis=2, keepdims=True)
    downstream = jnp.sum(jnp.where(lane == iota(shape, 1), jnp.broadcast_to(downstream, shape), 0.0), axis=1)
    part[0:TARGETS] = insulation
    part[8 : 8 + TARGETS] = upstream
    part_copies = [
        send(part, parts_in.at[m - 1], part_send.at[m - 1], part_recv.at[m - 1], at_band(m)) for m in range(1, BLOCKS + 1)
    ]
    for m, copy in enumerate(part_copies):
        receive(copy, place > m)
    flat = (TARGETS, 128)
    lane = iota(flat, 1)
    for m in range(1, BLOCKS + 1):
        turn = 128 - HEIGHT * m
        absent = float(HEIGHT) if m < BLOCKS else (HEIGHT - lane).astype(F32)
        insulation = insulation + jnp.where(place >= m, pltpu.roll(parts_in[m - 1, 0:TARGETS], turn, 1), 0.0)
        upstream = upstream + jnp.where(place >= m, pltpu.roll(parts_in[m - 1, 8 : 8 + TARGETS], turn, 1), absent)
    scores[:, 0, :] = (insulation * (1.0 / (STRIDE * STRIDE)))[:, :HEIGHT]
    scores[:, 1, :] = ((downstream - upstream) / (downstream + upstream))[:, :HEIGHT]
    for copy, there in sends:

        @pl.when(there)
        def _():
            copy.wait_send()


def hand_over(band, scores, band_hbm, scores_hbm, sems):
    copies = [pltpu.make_async_copy(a, b, sems.at[i]) for i, (a, b) in enumerate(((band, band_hbm), (scores, scores_hbm)))]
    for copy in copies:
        copy.start()
    for copy in copies:
        copy.wait()


def solution(mesh):
    genomes, towers = mesh.shape["genome"], mesh.shape["tower"]

    def per_device(bases, stitch, stem, trunk_in, trunk_out, pair, rate, conv, mix, head):
        anywhere = pl.BlockSpec(memory_space=pl.ANY)
        vmem = pltpu.VMEM
        dma = pltpu.SemaphoreType.DMA
        many = TARGETS * HEIGHT
        shapes = (
            jax.ShapeDtypeStruct((TARGETS, HEIGHT, BINS), F32),
            jax.ShapeDtypeStruct((TARGETS, 2, HEIGHT), F32),
        )
        in_vmem = pl.BlockSpec(memory_space=pltpu.VMEM)
        results = pl.pallas_call(
            functools.partial(kernel, genomes, towers),
            out_shape=shapes,
            in_specs=[anywhere] * 10,
            out_specs=(in_vmem, in_vmem),
            scratch_shapes=[
                vmem((1024, 128), jnp.int32),
                vmem((1, BINS), jnp.int32),
                vmem((C1, 4 * BP), BF16),
                vmem((TRUNK, MID, 3 * C1), BF16),
                vmem((TRUNK, MID, C1), BF16),
                vmem((2 * C2, C1), BF16),
                vmem((1, C2), F32),
                vmem((2, 3, C2, 3 * C2), BF16),
                vmem((2, C2, C2), BF16),
                vmem((TARGETS, C2), BF16),
                vmem((STRIDE, 4 * BP // CHUNKS), BF16),
                vmem((BLOCKS, STRIDE, 128), BF16),
                vmem((TRUNK, 3 * MID, C1), BF16),
                vmem((TRUNK, C1, MID), BF16),
                vmem((2, 3 * C2, 15 * C2), BF16),
                vmem((2, 3 * C2, 3 * C2), BF16),
                vmem((many, HEIGHT * C2), BF16),
                vmem((3, 24, BINS), F32),
                vmem((C2, 128), F32),
                vmem((BLOCKS + 1, HEIGHT, BINS), F32),
                vmem((C2, BINS), F32),
                vmem((2, C2, BINS), F32),
                vmem((20 * 144, 3 * BINS), BF16),
                vmem((18 * 144, 3 * BINS), BF16),
                vmem((18 * C2, 3 * BINS), F32),
                vmem((HEIGHT * C2, 3 * BINS), BF16),
                vmem((BLOCKS - 1, TARGETS, HEIGHT, BINS), BF16),
                vmem((BLOCKS - 1, TARGETS, HEIGHT, BINS), BF16),
                vmem((TARGETS, HEIGHT, BINS), F32),
                vmem((16, 128), F32),
                vmem((BLOCKS, 16, 128), F32),
                dma((9,)),
                dma((CHUNKS,)),
                dma((BLOCKS - 1,)),
                dma((BLOCKS - 1,)),
                dma((BLOCKS - 1,)),
                dma((BLOCKS - 1,)),
                dma((BLOCKS,)),
                dma((BLOCKS,)),
            ],
            compiler_params=pltpu.CompilerParams(collective_id=0, has_side_effects=True),
            name="contacts",
        )(
            bases.reshape(-1, 128),
            stitch.reshape(1, -1),
            stem,
            trunk_in,
            jnp.swapaxes(trunk_out, 1, 2),
            pair,
            rate.reshape(1, -1),
            conv,
            mix,
            head,
        )
        band, scores = pl.pallas_call(
            hand_over,
            out_shape=shapes,
            in_specs=[in_vmem, in_vmem],
            out_specs=(anywhere, anywhere),
            scratch_shapes=[dma((2,))],
            name="hand_over",
        )(*results)
        return band, jnp.swapaxes(scores, 0, 1)

    placed = (P("genome"), P(), P(), P(), P(), P(), P(), P(), P(), P())
    return jax.shard_map(
        per_device,
        mesh=mesh,
        in_specs=placed,
        out_specs=(P(None, ("genome", "tower"), None), P(None, None, ("genome", "tower"))),
        check_vma=False,
    )
```

```python
import functools

import jax
import jax.numpy as jnp
from jax import lax
from jax.experimental import pallas as pl
from jax.experimental.pallas import tpu as pltpu
from jax.sharding import PartitionSpec as P

BP = 2048
STRIDE = 64
BINS = 256
BLOCKS = 4
C1 = 96
MID = 48
C2 = 48
TARGETS = 5
TRUNK = 6
HEIGHT = 16
F32 = jnp.float32
BF16 = jnp.bfloat16
CHUNKS = 2
SPLIT = 124
MOVED = 136


def iota(shape, dim):
    return lax.broadcasted_iota(jnp.int32, shape, dim)


def dot(a, b):
    return jnp.dot(a, b, preferred_element_type=F32)


def shifted(value, starts, ends):
    width = value.shape[1]
    lane = iota(value.shape, 1)
    zero = jnp.zeros_like(value)
    before = pltpu.roll(value, 1, 1)
    after = pltpu.roll(value, width - 1, 1)
    for place in starts:
        before = jnp.where(lane == place, zero, before)
    for place in ends:
        after = jnp.where(lane == place, zero, after)
    return before, after


def kernel(
    genomes,
    towers,
    bases_hbm,
    stitch_hbm,
    stem_hbm,
    trunk_in_hbm,
    trunk_out_hbm,
    pair_hbm,
    rate_hbm,
    conv_hbm,
    mix_hbm,
    head_hbm,
    band,
    scores,
    bases,
    stitch,
    stem,
    trunk_in,
    trunk_out,
    pair,
    rate,
    conv,
    mix,
    head,
    window,
    taps,
    widen,
    wide_conv,
    wide_mix,
    wide_head,
    decay,
    rates,
    runs,
    row_weights,
    left,
    right,
    x1,
    x2,
    grid1,
    final,
    sent,
    landed,
    own_piece,
    part,
    parts_in,
    in_sems,
    stem_sems,
    feature_send,
    feature_recv,
    piece_send,
    piece_recv,
    part_send,
    part_recv,
):
    g = lax.axis_index("genome")
    t = lax.axis_index("tower")

    place = g * towers + t

    def at_genome(step):
        return {"genome": g + step, "tower": t}, jnp.logical_and(g + step >= 0, g + step < genomes)

    def at_band(step):
        up = lax.div(t + step + towers, towers) - 1
        near = {"genome": g + up, "tower": t + step - up * towers}
        return near, jnp.logical_and(place + step >= 0, place + step < genomes * towers)

    chunk = 4 * BP // CHUNKS
    bases_copy = pltpu.make_async_copy(bases_hbm, bases, in_sems.at[0])
    bases_copy.start()
    stem_copies = []
    for k in range(CHUNKS):
        lanes = pl.ds(k * chunk, chunk)
        stem_copies.append(pltpu.make_async_copy(stem_hbm.at[:, lanes], stem.at[:, lanes], stem_sems.at[k]))
        stem_copies[-1].start()
    small = [
        (stitch_hbm, stitch),
        (trunk_in_hbm, trunk_in),
        (trunk_out_hbm, trunk_out),
        (pair_hbm, pair),
        (rate_hbm, rate),
        (conv_hbm, conv),
        (mix_hbm, mix),
        (head_hbm, head),
    ]
    small_copies = [pltpu.make_async_copy(a, b, in_sems.at[i + 1]) for i, (a, b) in enumerate(small)]
    for copy in small_copies:
        copy.start()

    barrier = pltpu.get_barrier_semaphore()
    steps = (-1, 1, -2, 2, -3, 3)
    present = jnp.int32(0)
    for device, there in [at_genome(s) for s in steps] + [at_band(s) for s in steps]:
        present = present + there.astype(jnp.int32)

        @pl.when(there)
        def _():
            pl.semaphore_signal(barrier, inc=1, device_id=device, device_id_type=pl.DeviceIdType.MESH)

    bases_copy.wait()
    code = bases[pl.ds(0, STRIDE, stride=16), :]
    for k in range(1, 16):
        code = jnp.bitwise_or(code, lax.shift_left(bases[pl.ds(k, STRIDE, stride=16), :], jnp.int32(2 * k)))
    for copy in stem_copies:
        copy.wait()
    lane = iota((STRIDE, 128), 1)
    spread = [jnp.take_along_axis(code, lax.shift_right_logical(lane, 2) + 32 * m, axis=1) for m in range(4)]
    letter = jnp.bitwise_and(lane, 3)
    sums = []
    for k in range(16):
        mask = (3 << 2 * k) - (1 << 32 if k == 15 else 0)
        wanted = lax.shift_left(letter, jnp.int32(2 * k))
        hits = [jnp.where(jnp.bitwise_and(value, jnp.int32(mask)) == wanted, 1.0, 0.0) for value in spread]
        sums.append(
            lax.dot_general(
                jnp.concatenate(hits, axis=1).astype(BF16),
                stem[:, pl.ds(512 * k, 512)],
                (((1,), (1,)), ((), ())),
                preferred_element_type=F32,
            )
        )
    summed = sum(sums[1:], sums[0])
    window[0] = jnp.concatenate([summed, jnp.zeros((STRIDE, 128 - C1), F32)], axis=1).astype(BF16)

    pl.semaphore_wait(barrier, present)
    sends = []

    def send(source, target, send_sem, recv_sem, to):
        device, there = to
        copy = pltpu.make_async_remote_copy(
            src_ref=source,
            dst_ref=target,
            send_sem=send_sem,
            recv_sem=recv_sem,
            device_id=device,
            device_id_type=pl.DeviceIdType.MESH,
        )

        @pl.when(there)
        def _():
            copy.start()

        sends.append((copy, there))
        return copy

    def receive(copy, there):
        @pl.when(there)
        def _():
            copy.wait_recv()

    feature_copies = []
    for s in range(1, BLOCKS):
        feature_copies.append(
            send(window.at[0], window.at[s], feature_send.at[s - 1], feature_recv.at[s - 1], at_genome(-s))
        )

    for copy in small_copies:
        copy.wait()
    for l in range(TRUNK):
        for q in range(3):
            taps[l, pl.ds(q * MID, MID), :] = trunk_in[l, :, pl.ds(q * C1, C1)]
        widen[l] = trunk_out[l].astype(F32).T.astype(BF16)
    for l in range(2):
        for o in range(3):
            parts = []
            if o:
                parts.append(jnp.zeros((C2, 144 * o), BF16))
            parts += [conv[l, u] for u in range(3)]
            if o < 2:
                parts.append(jnp.zeros((C2, 144 * (2 - o)), BF16))
            wide_conv[l, pl.ds(o * C2, C2), :] = jnp.concatenate(parts, axis=1)
            parts = []
            if o:
                parts.append(jnp.zeros((C2, C2 * o), BF16))
            parts.append(mix[l])
            if o < 2:
                parts.append(jnp.zeros((C2, C2 * (2 - o)), BF16))
            wide_mix[l, pl.ds(o * C2, C2), :] = jnp.concatenate(parts, axis=1)
    lane = iota((C2, HEIGHT * C2), 1)
    row_of = lax.shift_right_logical(lane * 1366, 16)
    tile = jnp.where(lane - row_of * C2 == iota((C2, HEIGHT * C2), 0), 1.0, 0.0).astype(BF16)
    padded = jnp.concatenate([head[...].astype(F32), jnp.zeros((8 - TARGETS, C2), F32)], axis=0)
    head_rows = jnp.concatenate([padded] * HEIGHT, axis=0).astype(BF16)
    many = (8 * HEIGHT, HEIGHT * C2)
    row_of = lax.shift_right_logical(iota(many, 1) * 1366, 16)
    wide_head[...] = jnp.where(
        row_of == lax.shift_right_logical(iota(many, 0), 3), dot(head_rows, tile), 0.0
    ).astype(BF16)
    first_row = HEIGHT * t
    table = (24, BINS)
    lane = iota(table, 1)
    for tile in range(3):
        spot, col = STRIDE * tile, lane
        if tile == 2:
            spot, col = jnp.where(lane < SPLIT, 3 * STRIDE, 2 * STRIDE), jnp.where(lane < SPLIT, lane + MOVED, lane)
        rows = spot + first_row - 2 + iota(table, 0)
        gap = jnp.abs(rows - col).astype(F32)
        decay[tile] = jnp.where(jnp.logical_and(rows >= 0, rows < BINS), jnp.log(1.0 + gap), 1e30)
    span = (2 * 128, 128)
    ahead = jnp.bitwise_and(iota(span, 0), 127) - iota(span, 1)
    taken = jnp.logical_and(jnp.logical_and(ahead >= 1, ahead <= STRIDE), iota(span, 1) < STRIDE)
    runs[...] = jnp.where(taken, 1.0, 0.0).astype(BF16)
    square = (C2, C2)
    column = jnp.sum(
        jnp.where(iota(square, 0) == iota(square, 1), jnp.broadcast_to(rate[...], square), 0.0), axis=1, keepdims=True
    )
    rates[...] = jnp.broadcast_to(column, (C2, 128))
    band_shape = (HEIGHT, BINS)
    weights = jnp.broadcast_to(stitch[...].astype(F32), band_shape)
    lane = iota(band_shape, 1)
    row = iota(band_shape, 0)
    total = jnp.zeros(band_shape, F32)
    for b in range(BLOCKS):
        spot = STRIDE * b + first_row + row
        column = jnp.sum(jnp.where(lane == spot, weights, 0.0), axis=1, keepdims=True)
        column = jnp.broadcast_to(column, band_shape)
        inside = lane + spot < BINS
        row_weights[b] = jnp.where(inside, column, 0.0)
        total = total + jnp.where(jnp.logical_and(inside, g >= b), column, 0.0)
    row_weights[BLOCKS] = 1.0 / jnp.maximum(total, 1.0)

    for s, copy in enumerate(feature_copies):
        receive(copy, g + s + 1 < genomes)
    slots = [window[0].astype(F32)]
    for s in range(1, BLOCKS):
        slots.append(jnp.where(g + s < genomes, window[s].astype(F32), 0.0))
    stream = jnp.concatenate(slots, axis=0).T[:C1]
    lane = iota((MID, BINS), 1)
    for l in range(TRUNK):
        dilation = max(1, BINS // 2 ** (TRUNK - l))
        taken = dot(taps[l], jnp.maximum(stream, 0.0).astype(BF16))
        before = jnp.where(lane >= dilation, pltpu.roll(taken[:MID], dilation, 1), 0.0)
        after = jnp.where(lane < BINS - dilation, pltpu.roll(taken[2 * MID :], BINS - dilation, 1), 0.0)
        squeezed = jnp.maximum(before + taken[MID : 2 * MID] + after, 0.0).astype(BF16)
        stream = stream + dot(widen[l], squeezed)
    projected = dot(pair[...], jnp.maximum(stream, 0.0).astype(BF16))
    left[...] = pltpu.roll(projected[:C2], lax.rem(2 - first_row + BINS, BINS), 1)
    side = projected[C2:]
    right[0] = side
    right[1] = jnp.where(iota((C2, BINS), 1) < SPLIT, pltpu.roll(side, BINS - MOVED, 1), side)

    narrow = iota((C2, 128), 1) < SPLIT
    low = iota((C2, BINS), 1) < SPLIT

    def put(ref, at, value, tile):
        before, after = shifted(value, (0,) if tile == 0 else (), (BINS - 1, BINS - 1 - MOVED) if tile == 2 else (BINS - 1,))
        lanes = pl.ds(BINS * tile, BINS)
        ref[pl.ds(at, C2), lanes] = before
        ref[pl.ds(at + C2, C2), lanes] = value
        ref[pl.ds(at + 2 * C2, C2), lanes] = after

    def spread_column(at):
        return jnp.broadcast_to(left[:, at : at + 1], (C2, 128))

    def pair_row(r, tile):
        here = spread_column(STRIDE * tile + r)
        there = jnp.where(narrow, spread_column(3 * STRIDE + r), here) if tile == 2 else here
        decline = rates[...]
        halves = []
        for h, column in enumerate((there, here)):
            lanes = slice(128 * h, 128 * h + 128)
            fall = decline * jnp.broadcast_to(decay[tile, r : r + 1, lanes], (C2, 128))
            halves.append(jnp.maximum(column + right[tile // 2, :, lanes] - fall, 0.0))
        put(x1, 144 * r, jnp.concatenate(halves, axis=1).astype(BF16), tile)

    def convolve(l, ref, at, rows, tile):
        depth = 144 * (rows + 2)
        return dot(wide_conv[l, : C2 * rows, :depth], ref[pl.ds(144 * at, depth), pl.ds(BINS * tile, BINS)])

    def remix(l, convolved):
        rows = convolved.shape[0]
        return dot(wide_mix[l, :rows, :rows], jnp.maximum(convolved, 0.0).astype(BF16))

    def first_block(at, mixed, tile):
        for o in range(3):
            r = at + o + 1
            held = x1[pl.ds(144 * r + C2, C2), pl.ds(BINS * tile, BINS)].astype(F32)
            value = held + mixed[o * C2 : (o + 1) * C2]
            grid1[pl.ds(C2 * (r - 1), C2), pl.ds(BINS * tile, BINS)] = value
            value = jnp.maximum(value, 0.0)
            if tile == 0 and r == 1:
                value = jnp.where(t == 0, 0.0, value)
            if tile == 2 and r == HEIGHT + 2:
                value = jnp.where(jnp.logical_and(low, t == towers - 1), 0.0, value)
            put(x2, 144 * (r - 1), value.astype(BF16), tile)

    def second_block(at, mixed, tile):
        rows, lanes = mixed.shape[0], pl.ds(BINS * tile, BINS)
        value = grid1[pl.ds(C2 * (at + 1), rows), lanes] + mixed
        final[pl.ds(C2 * at, rows), lanes] = jnp.maximum(value, 0.0).astype(BF16)

    groups = ((0, 3), (3, 3), (6, 3), (9, 3), (12, 2), (14, 2))

    def tower(work):
        ones = [(tile, step, convolve(0, x1, 3 * step, 3, tile)) for tile, step in work if 0 <= step < 6]
        twos = [(tile, groups[step - 2], convolve(1, x2, *groups[step - 2], tile)) for tile, step in work if 2 <= step < 8]
        for tile, step in work:
            for r in range(3 * step + 5 if step >= 0 else 0, min(3 * step + 8, HEIGHT + 4) if step >= -1 else 0):
                pair_row(r, tile)
        ones = [(tile, step, remix(0, value)) for tile, step, value in ones]
        twos = [(tile, group, remix(1, value)) for tile, group, value in twos]
        for tile, step, value in ones:
            first_block(3 * step, value, tile)
        for tile, group, value in twos:
            second_block(group[0], value, tile)

    piece_copies = {}

    def piece_of(b, contact):
        start = STRIDE * b + first_row - (MOVED if b == 3 else 0)
        span = BINS if b < 2 else 128
        rows = []
        for r in range(HEIGHT):
            turned = pltpu.roll(contact[8 * r : 8 * r + 8], lax.rem(2 * BINS - r - start, BINS), 1)
            rows.append(turned[:, :span] * row_weights[b, r : r + 1, :span])
        return jnp.concatenate(rows, axis=0)

    def hand_on(b, piece):
        span = piece.shape[1]
        sent[b - 1, :, :span] = piece.astype(BF16)
        source, target = (ref.at[b - 1, :, pl.ds(0, span)] for ref in (sent, landed))
        piece_copies[b] = send(source, target, piece_send.at[b - 1], piece_recv.at[b - 1], at_genome(b))

    def contact_of(tile):
        return dot(wide_head[...], final[:, pl.ds(BINS * tile, BINS)])

    lags = (6,3,0)
    for moment in range(-1, lags[0] + 9):
        tower([(tile, moment - lags[tile]) for tile in (2, 1, 0)])
        if moment == lags[2] + 8:
            contact = contact_of(2)
            hand_on(3, piece_of(3, contact))
            hand_on(2, piece_of(2, contact))
        if moment == lags[1] + 8:
            hand_on(1, piece_of(1, contact_of(1)))
    own_piece[...] = piece_of(0, contact_of(0))

    for b, copy in piece_copies.items():
        receive(copy, g >= b)
    near = own_piece[:, :128]
    for b in range(1, BLOCKS):
        near = near + jnp.where(g >= b, landed[b - 1, :, :128].astype(F32), 0.0)
    far = own_piece[:, 128:] + jnp.where(g >= 1, landed[0, :, 128:].astype(F32), 0.0)
    near = [near[8 * r : 8 * r + 8] * row_weights[BLOCKS, r : r + 1, :128] for r in range(HEIGHT)]

    lane = iota((8, 128), 1)
    counted = jnp.logical_and(lane >= 1, lane <= STRIDE)
    joined = jnp.concatenate(near, axis=0)
    coarse = joined.astype(BF16)
    fine = (joined - coarse.astype(F32)).astype(BF16)
    squares = dot(jnp.concatenate([coarse, fine], axis=1), runs[...])
    insulation = upstream = downstream = jnp.zeros((8, 128), F32)
    for r in range(HEIGHT):
        insulation = insulation + pltpu.roll(squares[8 * r : 8 * r + 8], r, 1)
        contact = jnp.where(counted, jnp.exp(near[r]), 0.0)
        upstream = upstream + pltpu.roll(contact, r, 1)
        downstream = jnp.where(lane == r, jnp.sum(contact, axis=1, keepdims=True), downstream)
    part[0:8] = insulation
    part[8:16] = upstream
    part_copies = [
        send(part, parts_in.at[m - 1], part_send.at[m - 1], part_recv.at[m - 1], at_band(m)) for m in range(1, BLOCKS + 1)
    ]
    for r in range(HEIGHT):
        band[:, r, :128] = near[r][:TARGETS]
        band[:, r, 128:] = (far[8 * r : 8 * r + 8] * row_weights[BLOCKS, r : r + 1, 128:])[:TARGETS]
    for m, copy in enumerate(part_copies):
        receive(copy, place > m)
    for m in range(1, BLOCKS + 1):
        turn = 128 - HEIGHT * m
        absent = float(HEIGHT) if m < BLOCKS else (HEIGHT - lane).astype(F32)
        insulation = insulation + jnp.where(place >= m, pltpu.roll(parts_in[m - 1, 0:8], turn, 1), 0.0)
        upstream = upstream + jnp.where(place >= m, pltpu.roll(parts_in[m - 1, 8:16], turn, 1), absent)
    scores[:, 0, :] = (insulation * (1.0 / (STRIDE * STRIDE)))[:TARGETS, :HEIGHT]
    scores[:, 1, :] = ((downstream - upstream) / (downstream + upstream))[:TARGETS, :HEIGHT]
    for copy, there in sends:

        @pl.when(there)
        def _():
            copy.wait_send()


def hand_over(band, scores, band_hbm, scores_hbm, sems):
    copies = [pltpu.make_async_copy(a, b, sems.at[i]) for i, (a, b) in enumerate(((band, band_hbm), (scores, scores_hbm)))]
    for copy in copies:
        copy.start()
    for copy in copies:
        copy.wait()


def solution(mesh):
    genomes, towers = mesh.shape["genome"], mesh.shape["tower"]

    def per_device(bases, stitch, stem, trunk_in, trunk_out, pair, rate, conv, mix, head):
        anywhere = pl.BlockSpec(memory_space=pl.ANY)
        vmem = pltpu.VMEM
        dma = pltpu.SemaphoreType.DMA
        many = 8 * HEIGHT
        shapes = (
            jax.ShapeDtypeStruct((TARGETS, HEIGHT, BINS), F32),
            jax.ShapeDtypeStruct((TARGETS, 2, HEIGHT), F32),
        )
        in_vmem = pl.BlockSpec(memory_space=pltpu.VMEM)
        results = pl.pallas_call(
            functools.partial(kernel, genomes, towers),
            out_shape=shapes,
            in_specs=[anywhere] * 10,
            out_specs=(in_vmem, in_vmem),
            scratch_shapes=[
                vmem((1024, 128), jnp.int32),
                vmem((1, BINS), jnp.int32),
                vmem((C1, 4 * BP), BF16),
                vmem((TRUNK, MID, 3 * C1), BF16),
                vmem((TRUNK, MID, C1), BF16),
                vmem((2 * C2, C1), BF16),
                vmem((1, C2), F32),
                vmem((2, 3, C2, 3 * C2), BF16),
                vmem((2, C2, C2), BF16),
                vmem((TARGETS, C2), BF16),
                vmem((BLOCKS, STRIDE, 128), BF16),
                vmem((TRUNK, 3 * MID, C1), BF16),
                vmem((TRUNK, C1, MID), BF16),
                vmem((2, 3 * C2, 15 * C2), BF16),
                vmem((2, 3 * C2, 3 * C2), BF16),
                vmem((many, HEIGHT * C2), BF16),
                vmem((3, 24, BINS), F32),
                vmem((C2, 128), F32),
                vmem((2 * 128, 128), BF16),
                vmem((BLOCKS + 1, HEIGHT, BINS), F32),
                vmem((C2, BINS), F32),
                vmem((2, C2, BINS), F32),
                vmem((20 * 144, 3 * BINS), BF16),
                vmem((18 * 144, 3 * BINS), BF16),
                vmem((18 * C2, 3 * BINS), F32),
                vmem((HEIGHT * C2, 3 * BINS), BF16),
                vmem((BLOCKS - 1, many, BINS), BF16),
                vmem((BLOCKS - 1, many, BINS), BF16),
                vmem((many, BINS), F32),
                vmem((16, 128), F32),
                vmem((BLOCKS, 16, 128), F32),
                dma((9,)),
                dma((CHUNKS,)),
                dma((BLOCKS - 1,)),
                dma((BLOCKS - 1,)),
                dma((BLOCKS - 1,)),
                dma((BLOCKS - 1,)),
                dma((BLOCKS,)),
                dma((BLOCKS,)),
            ],
            compiler_params=pltpu.CompilerParams(collective_id=0, has_side_effects=True),
            name="contacts",
        )(
            bases.reshape(-1, 128),
            stitch.reshape(1, -1),
            stem,
            trunk_in,
            jnp.swapaxes(trunk_out, 1, 2),
            pair,
            rate.reshape(1, -1),
            conv,
            mix,
            head,
        )
        band, scores = pl.pallas_call(
            hand_over,
            out_shape=shapes,
            in_specs=[in_vmem, in_vmem],
            out_specs=(anywhere, anywhere),
            scratch_shapes=[dma((2,))],
            name="hand_over",
        )(*results)
        return band, jnp.swapaxes(scores, 0, 1)

    placed = (P("genome"), P(), P(), P(), P(), P(), P(), P(), P(), P())
    return jax.shard_map(
        per_device,
        mesh=mesh,
        in_specs=placed,
        out_specs=(P(None, ("genome", "tower"), None), P(None, None, ("genome", "tower"))),
        check_vma=False,
    )
```

```python
import functools

import jax
import jax.numpy as jnp
from jax import lax
from jax.experimental import pallas as pl
from jax.experimental.pallas import tpu as pltpu
from jax.sharding import PartitionSpec as P

BP = 2048
STRIDE = 64
BINS = 256
BLOCKS = 4
C1 = 96
MID = 48
C2 = 48
TARGETS = 5
TRUNK = 6
HEIGHT = 16
F32 = jnp.float32
BF16 = jnp.bfloat16
CHUNKS = 2
SPLIT = 124
MOVED = 136


def iota(shape, dim):
    return lax.broadcasted_iota(jnp.int32, shape, dim)


def dot(a, b):
    return jnp.dot(a, b, preferred_element_type=F32)


def shifted(value, starts, ends):
    width = value.shape[1]
    lane = iota(value.shape, 1)
    zero = jnp.zeros_like(value)
    before = pltpu.roll(value, 1, 1)
    after = pltpu.roll(value, width - 1, 1)
    for place in starts:
        before = jnp.where(lane == place, zero, before)
    for place in ends:
        after = jnp.where(lane == place, zero, after)
    return before, after


def kernel(
    genomes,
    towers,
    bases_hbm,
    stitch_hbm,
    stem_hbm,
    trunk_in_hbm,
    trunk_out_hbm,
    pair_hbm,
    rate_hbm,
    conv_hbm,
    mix_hbm,
    head_hbm,
    band,
    scores,
    bases,
    stitch,
    stem,
    trunk_in,
    trunk_out,
    pair,
    rate,
    conv,
    mix,
    head,
    window,
    taps,
    widen,
    wide_conv,
    wide_mix,
    wide_head,
    decay,
    rates,
    runs,
    row_weights,
    left,
    right,
    x1,
    x2,
    grid1,
    final,
    sent,
    landed,
    own_piece,
    part,
    parts_in,
    in_sems,
    stem_sems,
    feature_send,
    feature_recv,
    piece_send,
    piece_recv,
    part_send,
    part_recv,
):
    g = lax.axis_index("genome")
    t = lax.axis_index("tower")

    place = g * towers + t

    def at_genome(step):
        return {"genome": g + step, "tower": t}, jnp.logical_and(g + step >= 0, g + step < genomes)

    def at_band(step):
        up = lax.div(t + step + towers, towers) - 1
        near = {"genome": g + up, "tower": t + step - up * towers}
        return near, jnp.logical_and(place + step >= 0, place + step < genomes * towers)

    chunk = 4 * BP // CHUNKS
    bases_copy = pltpu.make_async_copy(bases_hbm, bases, in_sems.at[0])
    bases_copy.start()
    stem_copies = []
    for k in range(CHUNKS):
        lanes = pl.ds(k * chunk, chunk)
        stem_copies.append(pltpu.make_async_copy(stem_hbm.at[:, lanes], stem.at[:, lanes], stem_sems.at[k]))
        stem_copies[-1].start()
    small = [
        (stitch_hbm, stitch),
        (trunk_in_hbm, trunk_in),
        (trunk_out_hbm, trunk_out),
        (pair_hbm, pair),
        (rate_hbm, rate),
        (conv_hbm, conv),
        (mix_hbm, mix),
        (head_hbm, head),
    ]
    small_copies = [pltpu.make_async_copy(a, b, in_sems.at[i + 1]) for i, (a, b) in enumerate(small)]
    for copy in small_copies:
        copy.start()

    barrier = pltpu.get_barrier_semaphore()
    met = jnp.int32(towers - 1)
    for s in range(1, BLOCKS):
        met = met + (g >= s).astype(jnp.int32)
        device, there = at_genome(s)

        @pl.when(there)
        def _():
            pl.semaphore_signal(barrier, inc=1, device_id=device, device_id_type=pl.DeviceIdType.MESH)

    for s in range(1, towers):
        pl.semaphore_signal(
            barrier,
            inc=1,
            device_id={"genome": g, "tower": lax.rem(t + s, towers)},
            device_id_type=pl.DeviceIdType.MESH,
        )

    bases_copy.wait()
    code = bases[pl.ds(0, STRIDE, stride=16), :]
    for k in range(1, 16):
        code = jnp.bitwise_or(code, lax.shift_left(bases[pl.ds(k, STRIDE, stride=16), :], jnp.int32(2 * k)))
    for copy in stem_copies:
        copy.wait()
    lane = iota((STRIDE, 128), 1)
    spread = [jnp.take_along_axis(code, lax.shift_right_logical(lane, 2) + 32 * m, axis=1) for m in range(4)]
    letter = jnp.bitwise_and(lane, 3)
    sums = []
    for k in range(16):
        mask = (3 << 2 * k) - (1 << 32 if k == 15 else 0)
        wanted = lax.shift_left(letter, jnp.int32(2 * k))
        hits = [jnp.where(jnp.bitwise_and(value, jnp.int32(mask)) == wanted, 1.0, 0.0) for value in spread]
        sums.append(
            lax.dot_general(
                jnp.concatenate(hits, axis=1).astype(BF16),
                stem[:, pl.ds(512 * k, 512)],
                (((1,), (1,)), ((), ())),
                preferred_element_type=F32,
            )
        )
    summed = sum(sums[1:], sums[0])
    window[0] = jnp.concatenate([summed, jnp.zeros((STRIDE, 128 - C1), F32)], axis=1).astype(BF16)

    pl.semaphore_wait(barrier, met)
    sends = []

    def send(source, target, send_sem, recv_sem, to):
        device, there = to
        copy = pltpu.make_async_remote_copy(
            src_ref=source,
            dst_ref=target,
            send_sem=send_sem,
            recv_sem=recv_sem,
            device_id=device,
            device_id_type=pl.DeviceIdType.MESH,
        )

        @pl.when(there)
        def _():
            copy.start()

        sends.append((copy, there))
        return copy

    def receive(copy, there):
        @pl.when(there)
        def _():
            copy.wait_recv()

    feature_copies = []
    for s in range(1, BLOCKS):
        feature_copies.append(
            send(window.at[0], window.at[s], feature_send.at[s - 1], feature_recv.at[s - 1], at_genome(-s))
        )

    for copy in small_copies:
        copy.wait()
    for l in range(TRUNK):
        for q in range(3):
            taps[l, pl.ds(q * MID, MID), :] = trunk_in[l, :, pl.ds(q * C1, C1)]
        widen[l] = trunk_out[l].astype(F32).T.astype(BF16)
    for l in range(2):
        for o in range(3):
            parts = []
            if o:
                parts.append(jnp.zeros((C2, 144 * o), BF16))
            parts += [conv[l, u] for u in range(3)]
            if o < 2:
                parts.append(jnp.zeros((C2, 144 * (2 - o)), BF16))
            wide_conv[l, pl.ds(o * C2, C2), :] = jnp.concatenate(parts, axis=1)
            parts = []
            if o:
                parts.append(jnp.zeros((C2, C2 * o), BF16))
            parts.append(mix[l])
            if o < 2:
                parts.append(jnp.zeros((C2, C2 * (2 - o)), BF16))
            wide_mix[l, pl.ds(o * C2, C2), :] = jnp.concatenate(parts, axis=1)
    lane = iota((C2, HEIGHT * C2), 1)
    row_of = lax.shift_right_logical(lane * 1366, 16)
    tile = jnp.where(lane - row_of * C2 == iota((C2, HEIGHT * C2), 0), 1.0, 0.0).astype(BF16)
    padded = jnp.concatenate([head[...].astype(F32), jnp.zeros((8 - TARGETS, C2), F32)], axis=0)
    head_rows = jnp.concatenate([padded] * HEIGHT, axis=0).astype(BF16)
    many = (8 * HEIGHT, HEIGHT * C2)
    row_of = lax.shift_right_logical(iota(many, 1) * 1366, 16)
    wide_head[...] = jnp.where(
        row_of == lax.shift_right_logical(iota(many, 0), 3), dot(head_rows, tile), 0.0
    ).astype(BF16)
    first_row = HEIGHT * t
    table = (24, BINS)
    lane = iota(table, 1)
    for tile in range(3):
        spot, col = STRIDE * tile, lane
        if tile == 2:
            spot, col = jnp.where(lane < SPLIT, 3 * STRIDE, 2 * STRIDE), jnp.where(lane < SPLIT, lane + MOVED, lane)
        rows = spot + first_row - 2 + iota(table, 0)
        gap = jnp.abs(rows - col).astype(F32)
        decay[tile] = jnp.where(jnp.logical_and(rows >= 0, rows < BINS), jnp.log(1.0 + gap), 1e30)
    span = (2 * 128, 128)
    ahead = jnp.bitwise_and(iota(span, 0), 127) - iota(span, 1)
    taken = jnp.logical_and(jnp.logical_and(ahead >= 1, ahead <= STRIDE), iota(span, 1) < STRIDE)
    runs[...] = jnp.where(taken, 1.0, 0.0).astype(BF16)
    square = (C2, C2)
    column = jnp.sum(
        jnp.where(iota(square, 0) == iota(square, 1), jnp.broadcast_to(rate[...], square), 0.0), axis=1, keepdims=True
    )
    rates[...] = jnp.broadcast_to(column, (C2, 128))
    band_shape = (HEIGHT, BINS)
    weights = jnp.broadcast_to(stitch[...].astype(F32), band_shape)
    lane = iota(band_shape, 1)
    row = iota(band_shape, 0)
    total = jnp.zeros(band_shape, F32)
    for b in range(BLOCKS):
        spot = STRIDE * b + first_row + row
        column = jnp.sum(jnp.where(lane == spot, weights, 0.0), axis=1, keepdims=True)
        column = jnp.broadcast_to(column, band_shape)
        inside = lane + spot < BINS
        row_weights[b] = jnp.where(inside, column, 0.0)
        total = total + jnp.where(jnp.logical_and(inside, g >= b), column, 0.0)
    row_weights[BLOCKS] = 1.0 / jnp.maximum(total, 1.0)

    for s, copy in enumerate(feature_copies):
        receive(copy, g + s + 1 < genomes)
    slots = [window[0].astype(F32)]
    for s in range(1, BLOCKS):
        slots.append(jnp.where(g + s < genomes, window[s].astype(F32), 0.0))
    stream = jnp.concatenate(slots, axis=0).T[:C1]
    lane = iota((MID, BINS), 1)
    for l in range(TRUNK):
        dilation = max(1, BINS // 2 ** (TRUNK - l))
        taken = dot(taps[l], jnp.maximum(stream, 0.0).astype(BF16))
        before = jnp.where(lane >= dilation, pltpu.roll(taken[:MID], dilation, 1), 0.0)
        after = jnp.where(lane < BINS - dilation, pltpu.roll(taken[2 * MID :], BINS - dilation, 1), 0.0)
        squeezed = jnp.maximum(before + taken[MID : 2 * MID] + after, 0.0).astype(BF16)
        stream = stream + dot(widen[l], squeezed)
    projected = dot(pair[...], jnp.maximum(stream, 0.0).astype(BF16))
    left[...] = pltpu.roll(projected[:C2], lax.rem(2 - first_row + BINS, BINS), 1)
    side = projected[C2:]
    right[0] = side
    right[1] = jnp.where(iota((C2, BINS), 1) < SPLIT, pltpu.roll(side, BINS - MOVED, 1), side)

    narrow = iota((C2, 128), 1) < SPLIT
    low = iota((C2, BINS), 1) < SPLIT

    def put(ref, at, value, tile):
        before, after = shifted(value, (0,) if tile == 0 else (), (BINS - 1, BINS - 1 - MOVED) if tile == 2 else (BINS - 1,))
        lanes = pl.ds(BINS * tile, BINS)
        ref[pl.ds(at, C2), lanes] = before
        ref[pl.ds(at + C2, C2), lanes] = value
        ref[pl.ds(at + 2 * C2, C2), lanes] = after

    def spread_column(at):
        return jnp.broadcast_to(left[:, at : at + 1], (C2, 128))

    def pair_row(r, tile):
        here = spread_column(STRIDE * tile + r)
        there = jnp.where(narrow, spread_column(3 * STRIDE + r), here) if tile == 2 else here
        decline = rates[...]
        halves = []
        for h, column in enumerate((there, here)):
            lanes = slice(128 * h, 128 * h + 128)
            fall = decline * jnp.broadcast_to(decay[tile, r : r + 1, lanes], (C2, 128))
            halves.append(jnp.maximum(column + right[tile // 2, :, lanes] - fall, 0.0))
        put(x1, 144 * r, jnp.concatenate(halves, axis=1).astype(BF16), tile)

    def convolve(l, ref, at, rows, tile):
        depth = 144 * (rows + 2)
        return dot(wide_conv[l, : C2 * rows, :depth], ref[pl.ds(144 * at, depth), pl.ds(BINS * tile, BINS)])

    def remix(l, convolved):
        rows = convolved.shape[0]
        return dot(wide_mix[l, :rows, :rows], jnp.maximum(convolved, 0.0).astype(BF16))

    def first_block(at, mixed, tile):
        for o in range(3):
            r = at + o + 1
            held = x1[pl.ds(144 * r + C2, C2), pl.ds(BINS * tile, BINS)].astype(F32)
            value = held + mixed[o * C2 : (o + 1) * C2]
            grid1[pl.ds(C2 * (r - 1), C2), pl.ds(BINS * tile, BINS)] = value
            value = jnp.maximum(value, 0.0)
            if tile == 0 and r == 1:
                value = jnp.where(t == 0, 0.0, value)
            if tile == 2 and r == HEIGHT + 2:
                value = jnp.where(jnp.logical_and(low, t == towers - 1), 0.0, value)
            put(x2, 144 * (r - 1), value.astype(BF16), tile)

    def second_block(at, mixed, tile):
        rows, lanes = mixed.shape[0], pl.ds(BINS * tile, BINS)
        value = grid1[pl.ds(C2 * (at + 1), rows), lanes] + mixed
        final[pl.ds(C2 * at, rows), lanes] = jnp.maximum(value, 0.0).astype(BF16)

    groups = ((0, 3), (3, 3), (6, 3), (9, 3), (12, 2), (14, 2))

    def tower(work):
        ones = [(tile, step, convolve(0, x1, 3 * step, 3, tile)) for tile, step in work if 0 <= step < 6]
        twos = [(tile, groups[step - 2], convolve(1, x2, *groups[step - 2], tile)) for tile, step in work if 2 <= step < 8]
        for tile, step in work:
            for r in range(3 * step + 5 if step >= 0 else 0, min(3 * step + 8, HEIGHT + 4) if step >= -1 else 0):
                pair_row(r, tile)
        ones = [(tile, step, remix(0, value)) for tile, step, value in ones]
        twos = [(tile, group, remix(1, value)) for tile, group, value in twos]
        for tile, step, value in ones:
            first_block(3 * step, value, tile)
        for tile, group, value in twos:
            second_block(group[0], value, tile)

    piece_copies = {}

    def piece_of(b, contact):
        start = STRIDE * b + first_row - (MOVED if b == 3 else 0)
        span = BINS if b < 2 else 128
        rows = []
        for r in range(HEIGHT):
            turned = pltpu.roll(contact[8 * r : 8 * r + 8], lax.rem(2 * BINS - r - start, BINS), 1)
            rows.append(turned[:, :span] * row_weights[b, r : r + 1, :span])
        return jnp.concatenate(rows, axis=0)

    def hand_on(b, piece):
        span = piece.shape[1]
        sent[b - 1, :, :span] = piece.astype(BF16)
        source, target = (ref.at[b - 1, :, pl.ds(0, span)] for ref in (sent, landed))
        piece_copies[b] = send(source, target, piece_send.at[b - 1], piece_recv.at[b - 1], at_genome(b))

    def contact_of(tile):
        return dot(wide_head[...], final[:, pl.ds(BINS * tile, BINS)])

    lags = (6,0,0)
    for moment in range(-1, lags[0] + 9):
        tower([(tile, moment - lags[tile]) for tile in (2, 1, 0)])
        if moment == lags[2] + 8:
            contact = contact_of(2)
            hand_on(3, piece_of(3, contact))
            hand_on(2, piece_of(2, contact))
        if moment == lags[1] + 8:
            hand_on(1, piece_of(1, contact_of(1)))
    own_piece[...] = piece_of(0, contact_of(0))

    for b, copy in piece_copies.items():
        receive(copy, g >= b)
    near = own_piece[:, :128]
    for b in range(1, BLOCKS):
        near = near + jnp.where(g >= b, landed[b - 1, :, :128].astype(F32), 0.0)
    far = own_piece[:, 128:] + jnp.where(g >= 1, landed[0, :, 128:].astype(F32), 0.0)
    near = [near[8 * r : 8 * r + 8] * row_weights[BLOCKS, r : r + 1, :128] for r in range(HEIGHT)]

    lane = iota((8, 128), 1)
    counted = jnp.logical_and(lane >= 1, lane <= STRIDE)
    joined = jnp.concatenate(near, axis=0)
    coarse = joined.astype(BF16)
    fine = (joined - coarse.astype(F32)).astype(BF16)
    squares = dot(jnp.concatenate([coarse, fine], axis=1), runs[...])
    insulation = upstream = downstream = jnp.zeros((8, 128), F32)
    for r in range(HEIGHT):
        insulation = insulation + pltpu.roll(squares[8 * r : 8 * r + 8], r, 1)
        contact = jnp.where(counted, jnp.exp(near[r]), 0.0)
        upstream = upstream + pltpu.roll(contact, r, 1)
        downstream = jnp.where(lane == r, jnp.sum(contact, axis=1, keepdims=True), downstream)
    part[0:8] = insulation
    part[8:16] = upstream
    part_copies = [
        send(part, parts_in.at[m - 1], part_send.at[m - 1], part_recv.at[m - 1], at_band(m)) for m in range(1, BLOCKS + 1)
    ]
    for r in range(HEIGHT):
        band[:, r, :128] = near[r][:TARGETS]
        band[:, r, 128:] = (far[8 * r : 8 * r + 8] * row_weights[BLOCKS, r : r + 1, 128:])[:TARGETS]
    for m, copy in enumerate(part_copies):
        receive(copy, place > m)
    for m in range(1, BLOCKS + 1):
        turn = 128 - HEIGHT * m
        absent = float(HEIGHT) if m < BLOCKS else (HEIGHT - lane).astype(F32)
        insulation = insulation + jnp.where(place >= m, pltpu.roll(parts_in[m - 1, 0:8], turn, 1), 0.0)
        upstream = upstream + jnp.where(place >= m, pltpu.roll(parts_in[m - 1, 8:16], turn, 1), absent)
    scores[:, 0, :] = (insulation * (1.0 / (STRIDE * STRIDE)))[:TARGETS, :HEIGHT]
    scores[:, 1, :] = ((downstream - upstream) / (downstream + upstream))[:TARGETS, :HEIGHT]
    for copy, there in sends:

        @pl.when(there)
        def _():
            copy.wait_send()


def hand_over(band, scores, band_hbm, scores_hbm, sems):
    copies = [pltpu.make_async_copy(a, b, sems.at[i]) for i, (a, b) in enumerate(((band, band_hbm), (scores, scores_hbm)))]
    for copy in copies:
        copy.start()
    for copy in copies:
        copy.wait()


def solution(mesh):
    genomes, towers = mesh.shape["genome"], mesh.shape["tower"]

    def per_device(bases, stitch, stem, trunk_in, trunk_out, pair, rate, conv, mix, head):
        anywhere = pl.BlockSpec(memory_space=pl.ANY)
        vmem = pltpu.VMEM
        dma = pltpu.SemaphoreType.DMA
        many = 8 * HEIGHT
        shapes = (
            jax.ShapeDtypeStruct((TARGETS, HEIGHT, BINS), F32),
            jax.ShapeDtypeStruct((TARGETS, 2, HEIGHT), F32),
        )
        in_vmem = pl.BlockSpec(memory_space=pltpu.VMEM)
        results = pl.pallas_call(
            functools.partial(kernel, genomes, towers),
            out_shape=shapes,
            in_specs=[anywhere] * 10,
            out_specs=(in_vmem, in_vmem),
            scratch_shapes=[
                vmem((1024, 128), jnp.int32),
                vmem((1, BINS), jnp.int32),
                vmem((C1, 4 * BP), BF16),
                vmem((TRUNK, MID, 3 * C1), BF16),
                vmem((TRUNK, MID, C1), BF16),
                vmem((2 * C2, C1), BF16),
                vmem((1, C2), F32),
                vmem((2, 3, C2, 3 * C2), BF16),
                vmem((2, C2, C2), BF16),
                vmem((TARGETS, C2), BF16),
                vmem((BLOCKS, STRIDE, 128), BF16),
                vmem((TRUNK, 3 * MID, C1), BF16),
                vmem((TRUNK, C1, MID), BF16),
                vmem((2, 3 * C2, 15 * C2), BF16),
                vmem((2, 3 * C2, 3 * C2), BF16),
                vmem((many, HEIGHT * C2), BF16),
                vmem((3, 24, BINS), F32),
                vmem((C2, 128), F32),
                vmem((2 * 128, 128), BF16),
                vmem((BLOCKS + 1, HEIGHT, BINS), F32),
                vmem((C2, BINS), F32),
                vmem((2, C2, BINS), F32),
                vmem((20 * 144, 3 * BINS), BF16),
                vmem((18 * 144, 3 * BINS), BF16),
                vmem((18 * C2, 3 * BINS), F32),
                vmem((HEIGHT * C2, 3 * BINS), BF16),
                vmem((BLOCKS - 1, many, BINS), BF16),
                vmem((BLOCKS - 1, many, BINS), BF16),
                vmem((many, BINS), F32),
                vmem((16, 128), F32),
                vmem((BLOCKS, 16, 128), F32),
                dma((9,)),
                dma((CHUNKS,)),
                dma((BLOCKS - 1,)),
                dma((BLOCKS - 1,)),
                dma((BLOCKS - 1,)),
                dma((BLOCKS - 1,)),
                dma((BLOCKS,)),
                dma((BLOCKS,)),
            ],
            compiler_params=pltpu.CompilerParams(collective_id=0, has_side_effects=True),
            name="contacts",
        )(
            bases.reshape(-1, 128),
            stitch.reshape(1, -1),
            stem,
            trunk_in,
            jnp.swapaxes(trunk_out, 1, 2),
            pair,
            rate.reshape(1, -1),
            conv,
            mix,
            head,
        )
        band, scores = pl.pallas_call(
            hand_over,
            out_shape=shapes,
            in_specs=[in_vmem, in_vmem],
            out_specs=(anywhere, anywhere),
            scratch_shapes=[dma((2,))],
            name="hand_over",
        )(*results)
        return band, jnp.swapaxes(scores, 0, 1)

    placed = (P("genome"), P(), P(), P(), P(), P(), P(), P(), P(), P())
    return jax.shard_map(
        per_device,
        mesh=mesh,
        in_specs=placed,
        out_specs=(P(None, ("genome", "tower"), None), P(None, None, ("genome", "tower"))),
        check_vma=False,
    )
```

```python
import functools

import jax
import jax.numpy as jnp
from jax import lax
from jax.experimental import pallas as pl
from jax.experimental.pallas import tpu as pltpu
from jax.sharding import PartitionSpec as P

BP = 2048
STRIDE = 64
BINS = 256
BLOCKS = 4
C1 = 96
MID = 48
C2 = 48
TARGETS = 5
TRUNK = 6
HEIGHT = 16
F32 = jnp.float32
BF16 = jnp.bfloat16
CHUNKS = 2
SPLIT = 124
MOVED = 136


def iota(shape, dim):
    return lax.broadcasted_iota(jnp.int32, shape, dim)


def dot(a, b):
    return jnp.dot(a, b, preferred_element_type=F32)


def shifted(value, starts, ends):
    width = value.shape[1]
    lane = iota(value.shape, 1)
    zero = jnp.zeros_like(value)
    before = pltpu.roll(value, 1, 1)
    after = pltpu.roll(value, width - 1, 1)
    for place in starts:
        before = jnp.where(lane == place, zero, before)
    for place in ends:
        after = jnp.where(lane == place, zero, after)
    return before, after


def kernel(
    genomes,
    towers,
    bases_hbm,
    stitch_hbm,
    stem_hbm,
    trunk_in_hbm,
    trunk_out_hbm,
    pair_hbm,
    rate_hbm,
    conv_hbm,
    mix_hbm,
    head_hbm,
    band,
    scores,
    bases,
    stitch,
    stem,
    trunk_in,
    trunk_out,
    pair,
    rate,
    conv,
    mix,
    head,
    window,
    taps,
    widen,
    wide_conv,
    wide_mix,
    wide_head,
    decay,
    rates,
    runs,
    row_weights,
    left,
    right,
    x1,
    x2,
    grid1,
    final,
    sent,
    landed,
    squeeze,
    expand,
    own_piece,
    part,
    parts_in,
    in_sems,
    stem_sems,
    feature_send,
    feature_recv,
    piece_send,
    piece_recv,
    part_send,
    part_recv,
):
    g = lax.axis_index("genome")
    t = lax.axis_index("tower")

    place = g * towers + t

    def at_genome(step):
        return {"genome": g + step, "tower": t}, jnp.logical_and(g + step >= 0, g + step < genomes)

    def at_band(step):
        up = lax.div(t + step + towers, towers) - 1
        near = {"genome": g + up, "tower": t + step - up * towers}
        return near, jnp.logical_and(place + step >= 0, place + step < genomes * towers)

    chunk = 4 * BP // CHUNKS
    bases_copy = pltpu.make_async_copy(bases_hbm, bases, in_sems.at[0])
    bases_copy.start()
    stem_copies = []
    for k in range(CHUNKS):
        lanes = pl.ds(k * chunk, chunk)
        stem_copies.append(pltpu.make_async_copy(stem_hbm.at[:, lanes], stem.at[:, lanes], stem_sems.at[k]))
        stem_copies[-1].start()
    small = [
        (stitch_hbm, stitch),
        (trunk_in_hbm, trunk_in),
        (trunk_out_hbm, trunk_out),
        (pair_hbm, pair),
        (rate_hbm, rate),
        (conv_hbm, conv),
        (mix_hbm, mix),
        (head_hbm, head),
    ]
    small_copies = [pltpu.make_async_copy(a, b, in_sems.at[i + 1]) for i, (a, b) in enumerate(small)]
    for copy in small_copies:
        copy.start()

    barrier = pltpu.get_barrier_semaphore()
    met = jnp.int32(towers - 1)
    for s in range(1, BLOCKS):
        met = met + (g >= s).astype(jnp.int32)
        device, there = at_genome(s)

        @pl.when(there)
        def _():
            pl.semaphore_signal(barrier, inc=1, device_id=device, device_id_type=pl.DeviceIdType.MESH)

    for s in range(1, towers):
        pl.semaphore_signal(
            barrier,
            inc=1,
            device_id={"genome": g, "tower": lax.rem(t + s, towers)},
            device_id_type=pl.DeviceIdType.MESH,
        )

    bases_copy.wait()
    code = bases[pl.ds(0, STRIDE, stride=16), :]
    for k in range(1, 16):
        code = jnp.bitwise_or(code, lax.shift_left(bases[pl.ds(k, STRIDE, stride=16), :], jnp.int32(2 * k)))
    for copy in stem_copies:
        copy.wait()
    lane = iota((STRIDE, 128), 1)
    spread = [jnp.take_along_axis(code, lax.shift_right_logical(lane, 2) + 32 * m, axis=1) for m in range(4)]
    letter = jnp.bitwise_and(lane, 3)
    sums = []
    for k in range(16):
        mask = (3 << 2 * k) - (1 << 32 if k == 15 else 0)
        wanted = lax.shift_left(letter, jnp.int32(2 * k))
        hits = [jnp.where(jnp.bitwise_and(value, jnp.int32(mask)) == wanted, 1.0, 0.0) for value in spread]
        sums.append(
            lax.dot_general(
                jnp.concatenate(hits, axis=1).astype(BF16),
                stem[:, pl.ds(512 * k, 512)],
                (((1,), (1,)), ((), ())),
                preferred_element_type=F32,
            )
        )
    summed = sum(sums[1:], sums[0])
    window[0] = jnp.concatenate([summed, jnp.zeros((STRIDE, 128 - C1), F32)], axis=1).astype(BF16)

    pl.semaphore_wait(barrier, met)
    sends = []

    def send(source, target, send_sem, recv_sem, to):
        device, there = to
        copy = pltpu.make_async_remote_copy(
            src_ref=source,
            dst_ref=target,
            send_sem=send_sem,
            recv_sem=recv_sem,
            device_id=device,
            device_id_type=pl.DeviceIdType.MESH,
        )

        @pl.when(there)
        def _():
            copy.start()

        sends.append((copy, there))
        return copy

    def receive(copy, there):
        @pl.when(there)
        def _():
            copy.wait_recv()

    feature_copies = []
    for s in range(1, BLOCKS):
        feature_copies.append(
            send(window.at[0], window.at[s], feature_send.at[s - 1], feature_recv.at[s - 1], at_genome(-s))
        )

    for copy in small_copies:
        copy.wait()
    for l in range(TRUNK):
        for q in range(3):
            taps[l, pl.ds(q * MID, MID), :] = trunk_in[l, :, pl.ds(q * C1, C1)]
        widen[l] = trunk_out[l].astype(F32).T.astype(BF16)
    for l in range(2):
        for o in range(3):
            parts = []
            if o:
                parts.append(jnp.zeros((C2, 144 * o), BF16))
            parts += [conv[l, u] for u in range(3)]
            if o < 2:
                parts.append(jnp.zeros((C2, 144 * (2 - o)), BF16))
            wide_conv[l, pl.ds(o * C2, C2), :] = jnp.concatenate(parts, axis=1)
            parts = []
            if o:
                parts.append(jnp.zeros((C2, C2 * o), BF16))
            parts.append(mix[l])
            if o < 2:
                parts.append(jnp.zeros((C2, C2 * (2 - o)), BF16))
            wide_mix[l, pl.ds(o * C2, C2), :] = jnp.concatenate(parts, axis=1)
    lane = iota((C2, HEIGHT * C2), 1)
    row_of = lax.shift_right_logical(lane * 1366, 16)
    tile = jnp.where(lane - row_of * C2 == iota((C2, HEIGHT * C2), 0), 1.0, 0.0).astype(BF16)
    padded = jnp.concatenate([head[...].astype(F32), jnp.zeros((8 - TARGETS, C2), F32)], axis=0)
    head_rows = jnp.concatenate([padded] * HEIGHT, axis=0).astype(BF16)
    many = (8 * HEIGHT, HEIGHT * C2)
    row_of = lax.shift_right_logical(iota(many, 1) * 1366, 16)
    wide_head[...] = jnp.where(
        row_of == lax.shift_right_logical(iota(many, 0), 3), dot(head_rows, tile), 0.0
    ).astype(BF16)
    small = (TARGETS * HEIGHT, 8 * HEIGHT)
    row_of = lax.shift_right_logical(iota(small, 0) * 205, 10)
    squeeze[...] = jnp.where(iota(small, 1) == iota(small, 0) + 3 * row_of, 1.0, 0.0).astype(BF16)
    large = (8 * HEIGHT, 3 * TARGETS * HEIGHT)
    row, lane = iota(large, 0), iota(large, 1)
    lane = lane - TARGETS * HEIGHT * ((lane >= TARGETS * HEIGHT).astype(jnp.int32) + (lane >= 2 * TARGETS * HEIGHT).astype(jnp.int32))
    target = jnp.bitwise_and(row, 7)
    at = TARGETS * lax.shift_right_logical(row, 3) + target
    expand[...] = jnp.where(jnp.logical_and(target < TARGETS, lane == at), 1.0, 0.0).astype(BF16)
    first_row = HEIGHT * t
    table = (24, BINS)
    lane = iota(table, 1)
    for tile in range(3):
        spot, col = STRIDE * tile, lane
        if tile == 2:
            spot, col = jnp.where(lane < SPLIT, 3 * STRIDE, 2 * STRIDE), jnp.where(lane < SPLIT, lane + MOVED, lane)
        rows = spot + first_row - 2 + iota(table, 0)
        gap = jnp.abs(rows - col).astype(F32)
        decay[tile] = jnp.where(jnp.logical_and(rows >= 0, rows < BINS), jnp.log(1.0 + gap), 1e30)
    span = (2 * 128, 128)
    ahead = jnp.bitwise_and(iota(span, 0), 127) - iota(span, 1)
    taken = jnp.logical_and(jnp.logical_and(ahead >= 1, ahead <= STRIDE), iota(span, 1) < STRIDE)
    runs[...] = jnp.where(taken, 1.0, 0.0).astype(BF16)
    square = (C2, C2)
    column = jnp.sum(
        jnp.where(iota(square, 0) == iota(square, 1), jnp.broadcast_to(rate[...], square), 0.0), axis=1, keepdims=True
    )
    rates[...] = jnp.broadcast_to(column, (C2, 128))
    band_shape = (HEIGHT, BINS)
    weights = jnp.broadcast_to(stitch[...].astype(F32), band_shape)
    lane = iota(band_shape, 1)
    row = iota(band_shape, 0)
    total = jnp.zeros(band_shape, F32)
    for b in range(BLOCKS):
        spot = STRIDE * b + first_row + row
        column = jnp.sum(jnp.where(lane == spot, weights, 0.0), axis=1, keepdims=True)
        column = jnp.broadcast_to(column, band_shape)
        inside = lane + spot < BINS
        row_weights[b] = jnp.where(inside, column, 0.0)
        total = total + jnp.where(jnp.logical_and(inside, g >= b), column, 0.0)
    row_weights[BLOCKS] = 1.0 / jnp.maximum(total, 1.0)

    for s, copy in enumerate(feature_copies):
        receive(copy, g + s + 1 < genomes)
    slots = [window[0].astype(F32)]
    for s in range(1, BLOCKS):
        slots.append(jnp.where(g + s < genomes, window[s].astype(F32), 0.0))
    stream = jnp.concatenate(slots, axis=0).T[:C1]
    lane = iota((MID, BINS), 1)
    for l in range(TRUNK):
        dilation = max(1, BINS // 2 ** (TRUNK - l))
        taken = dot(taps[l], jnp.maximum(stream, 0.0).astype(BF16))
        before = jnp.where(lane >= dilation, pltpu.roll(taken[:MID], dilation, 1), 0.0)
        after = jnp.where(lane < BINS - dilation, pltpu.roll(taken[2 * MID :], BINS - dilation, 1), 0.0)
        squeezed = jnp.maximum(before + taken[MID : 2 * MID] + after, 0.0).astype(BF16)
        stream = stream + dot(widen[l], squeezed)
    projected = dot(pair[...], jnp.maximum(stream, 0.0).astype(BF16))
    left[...] = pltpu.roll(projected[:C2], lax.rem(2 - first_row + BINS, BINS), 1)
    side = projected[C2:]
    right[0] = side
    right[1] = jnp.where(iota((C2, BINS), 1) < SPLIT, pltpu.roll(side, BINS - MOVED, 1), side)

    narrow = iota((C2, 128), 1) < SPLIT
    low = iota((C2, BINS), 1) < SPLIT

    def put(ref, at, value, tile):
        before, after = shifted(value, (0,) if tile == 0 else (), (BINS - 1, BINS - 1 - MOVED) if tile == 2 else (BINS - 1,))
        lanes = pl.ds(BINS * tile, BINS)
        ref[pl.ds(at, C2), lanes] = before
        ref[pl.ds(at + C2, C2), lanes] = value
        ref[pl.ds(at + 2 * C2, C2), lanes] = after

    def spread_column(at):
        return jnp.broadcast_to(left[:, at : at + 1], (C2, 128))

    def pair_row(r, tile):
        here = spread_column(STRIDE * tile + r)
        there = jnp.where(narrow, spread_column(3 * STRIDE + r), here) if tile == 2 else here
        decline = rates[...]
        halves = []
        for h, column in enumerate((there, here)):
            lanes = slice(128 * h, 128 * h + 128)
            fall = decline * jnp.broadcast_to(decay[tile, r : r + 1, lanes], (C2, 128))
            halves.append(jnp.maximum(column + right[tile // 2, :, lanes] - fall, 0.0))
        put(x1, 144 * r, jnp.concatenate(halves, axis=1).astype(BF16), tile)

    def convolve(l, ref, at, rows, tile):
        depth = 144 * (rows + 2)
        return dot(wide_conv[l, : C2 * rows, :depth], ref[pl.ds(144 * at, depth), pl.ds(BINS * tile, BINS)])

    def remix(l, convolved):
        rows = convolved.shape[0]
        return dot(wide_mix[l, :rows, :rows], jnp.maximum(convolved, 0.0).astype(BF16))

    def first_block(at, mixed, tile):
        for o in range(3):
            r = at + o + 1
            held = x1[pl.ds(144 * r + C2, C2), pl.ds(BINS * tile, BINS)].astype(F32)
            value = held + mixed[o * C2 : (o + 1) * C2]
            grid1[pl.ds(C2 * (r - 1), C2), pl.ds(BINS * tile, BINS)] = value
            value = jnp.maximum(value, 0.0)
            if tile == 0 and r == 1:
                value = jnp.where(t == 0, 0.0, value)
            if tile == 2 and r == HEIGHT + 2:
                value = jnp.where(jnp.logical_and(low, t == towers - 1), 0.0, value)
            put(x2, 144 * (r - 1), value.astype(BF16), tile)

    def second_block(at, mixed, tile):
        rows, lanes = mixed.shape[0], pl.ds(BINS * tile, BINS)
        value = grid1[pl.ds(C2 * (at + 1), rows), lanes] + mixed
        final[pl.ds(C2 * at, rows), lanes] = jnp.maximum(value, 0.0).astype(BF16)

    groups = ((0, 3), (3, 3), (6, 3), (9, 3), (12, 2), (14, 2))

    def tower(work):
        ones = [(tile, step, convolve(0, x1, 3 * step, 3, tile)) for tile, step in work if 0 <= step < 6]
        twos = [(tile, groups[step - 2], convolve(1, x2, *groups[step - 2], tile)) for tile, step in work if 2 <= step < 8]
        for tile, step in work:
            for r in range(3 * step + 5 if step >= 0 else 0, min(3 * step + 8, HEIGHT + 4) if step >= -1 else 0):
                pair_row(r, tile)
        ones = [(tile, step, remix(0, value)) for tile, step, value in ones]
        twos = [(tile, group, remix(1, value)) for tile, group, value in twos]
        for tile, step, value in ones:
            first_block(3 * step, value, tile)
        for tile, group, value in twos:
            second_block(group[0], value, tile)

    piece_copies = {}

    def piece_of(b, contact):
        start = STRIDE * b + first_row - (MOVED if b == 3 else 0)
        span = BINS if b < 2 else 128
        rows = []
        for r in range(HEIGHT):
            turned = pltpu.roll(contact[8 * r : 8 * r + 8], lax.rem(2 * BINS - r - start, BINS), 1)
            rows.append(turned[:, :span] * row_weights[b, r : r + 1, :span])
        return jnp.concatenate(rows, axis=0)

    def hand_on(b, piece):
        span = piece.shape[1]
        sent[b - 1, :, :span] = dot(squeeze[...], piece.astype(BF16)).astype(BF16)
        source = sent.at[b - 1, :, pl.ds(0, span)]
        target = landed.at[pl.ds(TARGETS * HEIGHT * (b - 1), TARGETS * HEIGHT), pl.ds(0, span)]
        piece_copies[b] = send(source, target, piece_send.at[b - 1], piece_recv.at[b - 1], at_genome(b))

    def contact_of(tile):
        return dot(wide_head[...], final[:, pl.ds(BINS * tile, BINS)])

    lags = (9,0,0)
    for moment in range(-1, lags[0] + 9):
        tower([(tile, moment - lags[tile]) for tile in (2, 1, 0)])
        if moment == lags[1] + 8:
            hand_on(1, piece_of(1, contact_of(1)))
            contact = contact_of(2)
            hand_on(3, piece_of(3, contact))
            hand_on(2, piece_of(2, contact))
    own_piece[...] = piece_of(0, contact_of(0))

    for b, copy in piece_copies.items():
        receive(copy, g >= b)
    rows = TARGETS * HEIGHT
    arrived = jnp.concatenate(
        [jnp.where(g >= b, landed[rows * (b - 1) : rows * b, :128].astype(F32), 0.0) for b in range(1, BLOCKS)], axis=0
    )
    near = own_piece[:, :128] + dot(expand[...], arrived.astype(BF16))
    arrived = jnp.where(g >= 1, landed[:rows, 128:].astype(F32), 0.0)
    near = [near[8 * r : 8 * r + 8] * row_weights[BLOCKS, r : r + 1, :128] for r in range(HEIGHT)]

    lane = iota((8, 128), 1)
    counted = jnp.logical_and(lane >= 1, lane <= STRIDE)
    joined = jnp.concatenate(near, axis=0)
    coarse = joined.astype(BF16)
    fine = (joined - coarse.astype(F32)).astype(BF16)
    squares = dot(jnp.concatenate([coarse, fine], axis=1), runs[...])
    insulation = upstream = downstream = jnp.zeros((8, 128), F32)
    for r in range(HEIGHT):
        insulation = insulation + pltpu.roll(squares[8 * r : 8 * r + 8], r, 1)
        contact = jnp.where(counted, jnp.exp(near[r]), 0.0)
        upstream = upstream + pltpu.roll(contact, r, 1)
        downstream = jnp.where(lane == r, jnp.sum(contact, axis=1, keepdims=True), downstream)
    part[0:8] = insulation
    part[8:16] = upstream
    part_copies = [
        send(part, parts_in.at[m - 1], part_send.at[m - 1], part_recv.at[m - 1], at_band(m)) for m in range(1, BLOCKS + 1)
    ]
    far = own_piece[:, 128:] + dot(expand[:, :rows], arrived.astype(BF16))
    for r in range(HEIGHT):
        band[:, r, :128] = near[r][:TARGETS]
        band[:, r, 128:] = (far[8 * r : 8 * r + 8] * row_weights[BLOCKS, r : r + 1, 128:])[:TARGETS]
    for m, copy in enumerate(part_copies):
        receive(copy, place > m)
    for m in range(1, BLOCKS + 1):
        turn = 128 - HEIGHT * m
        absent = float(HEIGHT) if m < BLOCKS else (HEIGHT - lane).astype(F32)
        insulation = insulation + jnp.where(place >= m, pltpu.roll(parts_in[m - 1, 0:8], turn, 1), 0.0)
        upstream = upstream + jnp.where(place >= m, pltpu.roll(parts_in[m - 1, 8:16], turn, 1), absent)
    scores[:, 0, :] = (insulation * (1.0 / (STRIDE * STRIDE)))[:TARGETS, :HEIGHT]
    scores[:, 1, :] = ((downstream - upstream) / (downstream + upstream))[:TARGETS, :HEIGHT]
    for copy, there in sends:

        @pl.when(there)
        def _():
            copy.wait_send()


def hand_over(band, scores, band_hbm, scores_hbm, sems):
    copies = [pltpu.make_async_copy(a, b, sems.at[i]) for i, (a, b) in enumerate(((band, band_hbm), (scores, scores_hbm)))]
    for copy in copies:
        copy.start()
    for copy in copies:
        copy.wait()


def solution(mesh):
    genomes, towers = mesh.shape["genome"], mesh.shape["tower"]

    def per_device(bases, stitch, stem, trunk_in, trunk_out, pair, rate, conv, mix, head):
        anywhere = pl.BlockSpec(memory_space=pl.ANY)
        vmem = pltpu.VMEM
        dma = pltpu.SemaphoreType.DMA
        many = 8 * HEIGHT
        shapes = (
            jax.ShapeDtypeStruct((TARGETS, HEIGHT, BINS), F32),
            jax.ShapeDtypeStruct((TARGETS, 2, HEIGHT), F32),
        )
        in_vmem = pl.BlockSpec(memory_space=pltpu.VMEM)
        results = pl.pallas_call(
            functools.partial(kernel, genomes, towers),
            out_shape=shapes,
            in_specs=[anywhere] * 10,
            out_specs=(in_vmem, in_vmem),
            scratch_shapes=[
                vmem((1024, 128), jnp.int32),
                vmem((1, BINS), jnp.int32),
                vmem((C1, 4 * BP), BF16),
                vmem((TRUNK, MID, 3 * C1), BF16),
                vmem((TRUNK, MID, C1), BF16),
                vmem((2 * C2, C1), BF16),
                vmem((1, C2), F32),
                vmem((2, 3, C2, 3 * C2), BF16),
                vmem((2, C2, C2), BF16),
                vmem((TARGETS, C2), BF16),
                vmem((BLOCKS, STRIDE, 128), BF16),
                vmem((TRUNK, 3 * MID, C1), BF16),
                vmem((TRUNK, C1, MID), BF16),
                vmem((2, 3 * C2, 15 * C2), BF16),
                vmem((2, 3 * C2, 3 * C2), BF16),
                vmem((many, HEIGHT * C2), BF16),
                vmem((3, 24, BINS), F32),
                vmem((C2, 128), F32),
                vmem((2 * 128, 128), BF16),
                vmem((BLOCKS + 1, HEIGHT, BINS), F32),
                vmem((C2, BINS), F32),
                vmem((2, C2, BINS), F32),
                vmem((20 * 144, 3 * BINS), BF16),
                vmem((18 * 144, 3 * BINS), BF16),
                vmem((18 * C2, 3 * BINS), F32),
                vmem((HEIGHT * C2, 3 * BINS), BF16),
                vmem((BLOCKS - 1, TARGETS * HEIGHT, BINS), BF16),
                vmem(((BLOCKS - 1) * TARGETS * HEIGHT, BINS), BF16),
                vmem((TARGETS * HEIGHT, many), BF16),
                vmem((many, 3 * TARGETS * HEIGHT), BF16),
                vmem((many, BINS), F32),
                vmem((16, 128), F32),
                vmem((BLOCKS, 16, 128), F32),
                dma((9,)),
                dma((CHUNKS,)),
                dma((BLOCKS - 1,)),
                dma((BLOCKS - 1,)),
                dma((BLOCKS - 1,)),
                dma((BLOCKS - 1,)),
                dma((BLOCKS,)),
                dma((BLOCKS,)),
            ],
            compiler_params=pltpu.CompilerParams(collective_id=0, has_side_effects=True),
            name="contacts",
        )(
            bases.reshape(-1, 128),
            stitch.reshape(1, -1),
            stem,
            trunk_in,
            jnp.swapaxes(trunk_out, 1, 2),
            pair,
            rate.reshape(1, -1),
            conv,
            mix,
            head,
        )
        band, scores = pl.pallas_call(
            hand_over,
            out_shape=shapes,
            in_specs=[in_vmem, in_vmem],
            out_specs=(anywhere, anywhere),
            scratch_shapes=[dma((2,))],
            name="hand_over",
        )(*results)
        return band, jnp.swapaxes(scores, 0, 1)

    placed = (P("genome"), P(), P(), P(), P(), P(), P(), P(), P(), P())
    return jax.shard_map(
        per_device,
        mesh=mesh,
        in_specs=placed,
        out_specs=(P(None, ("genome", "tower"), None), P(None, None, ("genome", "tower"))),
        check_vma=False,
    )
```

```python
import functools

import jax
import jax.numpy as jnp
from jax import lax
from jax.experimental import pallas as pl
from jax.experimental.pallas import tpu as pltpu
from jax.sharding import PartitionSpec as P

BP = 2048
STRIDE = 64
BINS = 256
BLOCKS = 4
C1 = 96
MID = 48
C2 = 48
TARGETS = 5
TRUNK = 6
HEIGHT = 16
F32 = jnp.float32
BF16 = jnp.bfloat16
CHUNKS = 2
SPLIT = 124
MOVED = 136


def iota(shape, dim):
    return lax.broadcasted_iota(jnp.int32, shape, dim)


def dot(a, b):
    return jnp.dot(a, b, preferred_element_type=F32)


def shifted(value, starts, ends):
    width = value.shape[1]
    lane = iota(value.shape, 1)
    zero = jnp.zeros_like(value)
    before = pltpu.roll(value, 1, 1)
    after = pltpu.roll(value, width - 1, 1)
    for place in starts:
        before = jnp.where(lane == place, zero, before)
    for place in ends:
        after = jnp.where(lane == place, zero, after)
    return before, after


def kernel(
    genomes,
    towers,
    bases_hbm,
    stitch_hbm,
    stem_hbm,
    trunk_in_hbm,
    trunk_out_hbm,
    pair_hbm,
    rate_hbm,
    conv_hbm,
    mix_hbm,
    head_hbm,
    band,
    scores,
    bases,
    stitch,
    stem,
    trunk_in,
    trunk_out,
    pair,
    rate,
    conv,
    mix,
    head,
    window,
    taps,
    widen,
    wide_conv,
    wide_mix,
    wide_head,
    decay,
    rates,
    runs,
    row_weights,
    left,
    right,
    x1,
    x2,
    grid1,
    final,
    sent,
    landed,
    squeeze,
    expand,
    own_piece,
    part,
    parts_in,
    in_sems,
    stem_sems,
    feature_send,
    feature_recv,
    piece_send,
    piece_recv,
    part_send,
    part_recv,
):
    g = lax.axis_index("genome")
    t = lax.axis_index("tower")

    place = g * towers + t

    def at_genome(step):
        return {"genome": g + step, "tower": t}, jnp.logical_and(g + step >= 0, g + step < genomes)

    def at_band(step):
        up = lax.div(t + step + towers, towers) - 1
        near = {"genome": g + up, "tower": t + step - up * towers}
        return near, jnp.logical_and(place + step >= 0, place + step < genomes * towers)

    chunk = 4 * BP // CHUNKS
    bases_copy = pltpu.make_async_copy(bases_hbm, bases, in_sems.at[0])
    bases_copy.start()
    stem_copies = []
    for k in range(CHUNKS):
        lanes = pl.ds(k * chunk, chunk)
        stem_copies.append(pltpu.make_async_copy(stem_hbm.at[:, lanes], stem.at[:, lanes], stem_sems.at[k]))
        stem_copies[-1].start()
    small = [
        (stitch_hbm, stitch),
        (trunk_in_hbm, trunk_in),
        (trunk_out_hbm, trunk_out),
        (pair_hbm, pair),
        (rate_hbm, rate),
        (conv_hbm, conv),
        (mix_hbm, mix),
        (head_hbm, head),
    ]
    small_copies = [pltpu.make_async_copy(a, b, in_sems.at[i + 1]) for i, (a, b) in enumerate(small)]
    for copy in small_copies:
        copy.start()

    barrier = pltpu.get_barrier_semaphore()
    met = jnp.int32(towers - 1)
    for s in range(1, BLOCKS):
        met = met + (g >= s).astype(jnp.int32)
        device, there = at_genome(s)

        @pl.when(there)
        def _():
            pl.semaphore_signal(barrier, inc=1, device_id=device, device_id_type=pl.DeviceIdType.MESH)

    for s in range(1, towers):
        pl.semaphore_signal(
            barrier,
            inc=1,
            device_id={"genome": g, "tower": lax.rem(t + s, towers)},
            device_id_type=pl.DeviceIdType.MESH,
        )

    bases_copy.wait()
    code = bases[pl.ds(0, STRIDE, stride=16), :]
    for k in range(1, 16):
        code = jnp.bitwise_or(code, lax.shift_left(bases[pl.ds(k, STRIDE, stride=16), :], jnp.int32(2 * k)))
    for copy in stem_copies:
        copy.wait()
    lane = iota((STRIDE, 128), 1)
    spread = [jnp.take_along_axis(code, lax.shift_right_logical(lane, 2) + 32 * m, axis=1) for m in range(4)]
    letter = jnp.bitwise_and(lane, 3)
    sums = []
    for k in range(16):
        mask = (3 << 2 * k) - (1 << 32 if k == 15 else 0)
        wanted = lax.shift_left(letter, jnp.int32(2 * k))
        hits = [jnp.where(jnp.bitwise_and(value, jnp.int32(mask)) == wanted, 1.0, 0.0) for value in spread]
        sums.append(
            lax.dot_general(
                jnp.concatenate(hits, axis=1).astype(BF16),
                stem[:, pl.ds(512 * k, 512)],
                (((1,), (1,)), ((), ())),
                preferred_element_type=F32,
            )
        )
    summed = sum(sums[1:], sums[0])
    window[0] = jnp.concatenate([summed, jnp.zeros((STRIDE, 128 - C1), F32)], axis=1).astype(BF16)

    pl.semaphore_wait(barrier, met)
    sends = []

    def send(source, target, send_sem, recv_sem, to):
        device, there = to
        copy = pltpu.make_async_remote_copy(
            src_ref=source,
            dst_ref=target,
            send_sem=send_sem,
            recv_sem=recv_sem,
            device_id=device,
            device_id_type=pl.DeviceIdType.MESH,
        )

        @pl.when(there)
        def _():
            copy.start()

        sends.append((copy, there))
        return copy

    def receive(copy, there):
        @pl.when(there)
        def _():
            copy.wait_recv()

    feature_copies = []
    for s in range(1, BLOCKS):
        feature_copies.append(
            send(window.at[0], window.at[s], feature_send.at[s - 1], feature_recv.at[s - 1], at_genome(-s))
        )

    for copy in small_copies:
        copy.wait()
    for l in range(TRUNK):
        for q in range(3):
            taps[l, pl.ds(q * MID, MID), :] = trunk_in[l, :, pl.ds(q * C1, C1)]
        widen[l] = trunk_out[l].astype(F32).T.astype(BF16)
    for l in range(2):
        for o in range(3):
            parts = []
            if o:
                parts.append(jnp.zeros((C2, 144 * o), BF16))
            parts += [conv[l, u] for u in range(3)]
            if o < 2:
                parts.append(jnp.zeros((C2, 144 * (2 - o)), BF16))
            wide_conv[l, pl.ds(o * C2, C2), :] = jnp.concatenate(parts, axis=1)
            parts = []
            if o:
                parts.append(jnp.zeros((C2, C2 * o), BF16))
            parts.append(mix[l])
            if o < 2:
                parts.append(jnp.zeros((C2, C2 * (2 - o)), BF16))
            wide_mix[l, pl.ds(o * C2, C2), :] = jnp.concatenate(parts, axis=1)
    lane = iota((C2, HEIGHT * C2), 1)
    row_of = lax.shift_right_logical(lane * 1366, 16)
    tile = jnp.where(lane - row_of * C2 == iota((C2, HEIGHT * C2), 0), 1.0, 0.0).astype(BF16)
    padded = jnp.concatenate([head[...].astype(F32), jnp.zeros((8 - TARGETS, C2), F32)], axis=0)
    head_rows = jnp.concatenate([padded] * HEIGHT, axis=0).astype(BF16)
    many = (8 * HEIGHT, HEIGHT * C2)
    row_of = lax.shift_right_logical(iota(many, 1) * 1366, 16)
    wide_head[...] = jnp.where(
        row_of == lax.shift_right_logical(iota(many, 0), 3), dot(head_rows, tile), 0.0
    ).astype(BF16)
    small = (TARGETS * HEIGHT, 8 * HEIGHT)
    row_of = lax.shift_right_logical(iota(small, 0) * 205, 10)
    squeeze[...] = jnp.where(iota(small, 1) == iota(small, 0) + 3 * row_of, 1.0, 0.0).astype(BF16)
    large = (8 * HEIGHT, 3 * TARGETS * HEIGHT)
    row, lane = iota(large, 0), iota(large, 1)
    lane = lane - TARGETS * HEIGHT * ((lane >= TARGETS * HEIGHT).astype(jnp.int32) + (lane >= 2 * TARGETS * HEIGHT).astype(jnp.int32))
    target = jnp.bitwise_and(row, 7)
    at = TARGETS * lax.shift_right_logical(row, 3) + target
    expand[...] = jnp.where(jnp.logical_and(target < TARGETS, lane == at), 1.0, 0.0).astype(BF16)
    first_row = HEIGHT * t
    table = (24, BINS)
    lane = iota(table, 1)
    for tile in range(3):
        spot, col = STRIDE * tile, lane
        if tile == 2:
            spot, col = jnp.where(lane < SPLIT, 3 * STRIDE, 2 * STRIDE), jnp.where(lane < SPLIT, lane + MOVED, lane)
        rows = spot + first_row - 2 + iota(table, 0)
        gap = jnp.abs(rows - col).astype(F32)
        decay[tile] = jnp.where(jnp.logical_and(rows >= 0, rows < BINS), jnp.log(1.0 + gap), 1e30)
    span = (2 * 128, 128)
    ahead = jnp.bitwise_and(iota(span, 0), 127) - iota(span, 1)
    taken = jnp.logical_and(jnp.logical_and(ahead >= 1, ahead <= STRIDE), iota(span, 1) < STRIDE)
    runs[...] = jnp.where(taken, 1.0, 0.0).astype(BF16)
    square = (C2, C2)
    column = jnp.sum(
        jnp.where(iota(square, 0) == iota(square, 1), jnp.broadcast_to(rate[...], square), 0.0), axis=1, keepdims=True
    )
    rates[...] = jnp.broadcast_to(column, (C2, 128))
    band_shape = (HEIGHT, BINS)
    weights = jnp.broadcast_to(stitch[...].astype(F32), band_shape)
    lane = iota(band_shape, 1)
    row = iota(band_shape, 0)
    total = jnp.zeros(band_shape, F32)
    for b in range(BLOCKS):
        spot = STRIDE * b + first_row + row
        column = jnp.sum(jnp.where(lane == spot, weights, 0.0), axis=1, keepdims=True)
        column = jnp.broadcast_to(column, band_shape)
        inside = lane + spot < BINS
        row_weights[b] = jnp.where(inside, column, 0.0)
        total = total + jnp.where(jnp.logical_and(inside, g >= b), column, 0.0)
    row_weights[BLOCKS] = 1.0 / jnp.maximum(total, 1.0)

    for s, copy in enumerate(feature_copies):
        receive(copy, g + s + 1 < genomes)
    slots = [window[0].astype(F32)]
    for s in range(1, BLOCKS):
        slots.append(jnp.where(g + s < genomes, window[s].astype(F32), 0.0))
    stream = jnp.concatenate(slots, axis=0).T[:C1]
    lane = iota((MID, BINS), 1)
    for l in range(TRUNK):
        dilation = max(1, BINS // 2 ** (TRUNK - l))
        taken = dot(taps[l], jnp.maximum(stream, 0.0).astype(BF16))
        before = jnp.where(lane >= dilation, pltpu.roll(taken[:MID], dilation, 1), 0.0)
        after = jnp.where(lane < BINS - dilation, pltpu.roll(taken[2 * MID :], BINS - dilation, 1), 0.0)
        squeezed = jnp.maximum(before + taken[MID : 2 * MID] + after, 0.0).astype(BF16)
        stream = stream + dot(widen[l], squeezed)
    projected = dot(pair[...], jnp.maximum(stream, 0.0).astype(BF16))
    left[...] = pltpu.roll(projected[:C2], lax.rem(2 - first_row + BINS, BINS), 1)
    side = projected[C2:]
    right[0] = side
    right[1] = jnp.where(iota((C2, BINS), 1) < SPLIT, pltpu.roll(side, BINS - MOVED, 1), side)

    narrow = iota((C2, 128), 1) < SPLIT
    low = iota((C2, BINS), 1) < SPLIT

    def put(ref, at, value, tile):
        before, after = shifted(value, (0,) if tile == 0 else (), (BINS - 1, BINS - 1 - MOVED) if tile == 2 else (BINS - 1,))
        lanes = pl.ds(BINS * tile, BINS)
        ref[pl.ds(at, C2), lanes] = before
        ref[pl.ds(at + C2, C2), lanes] = value
        ref[pl.ds(at + 2 * C2, C2), lanes] = after

    def spread_column(at):
        return jnp.broadcast_to(left[:, at : at + 1], (C2, 128))

    def pair_row(r, tile):
        here = spread_column(STRIDE * tile + r)
        there = jnp.where(narrow, spread_column(3 * STRIDE + r), here) if tile == 2 else here
        decline = rates[...]
        halves = []
        for h, column in enumerate((there, here)):
            lanes = slice(128 * h, 128 * h + 128)
            fall = decline * jnp.broadcast_to(decay[tile, r : r + 1, lanes], (C2, 128))
            halves.append(jnp.maximum(column + right[tile // 2, :, lanes] - fall, 0.0))
        put(x1, 144 * r, jnp.concatenate(halves, axis=1).astype(BF16), tile)

    def convolve(l, ref, at, rows, tile):
        depth = 144 * (rows + 2)
        return dot(wide_conv[l, : C2 * rows, :depth], ref[pl.ds(144 * at, depth), pl.ds(BINS * tile, BINS)])

    def remix(l, convolved):
        rows = convolved.shape[0]
        return dot(wide_mix[l, :rows, :rows], jnp.maximum(convolved, 0.0).astype(BF16))

    def first_block(at, mixed, tile):
        for o in range(3):
            r = at + o + 1
            held = x1[pl.ds(144 * r + C2, C2), pl.ds(BINS * tile, BINS)].astype(F32)
            value = held + mixed[o * C2 : (o + 1) * C2]
            grid1[pl.ds(C2 * (r - 1), C2), pl.ds(BINS * tile, BINS)] = value
            value = jnp.maximum(value, 0.0)
            if tile == 0 and r == 1:
                value = jnp.where(t == 0, 0.0, value)
            if tile == 2 and r == HEIGHT + 2:
                value = jnp.where(jnp.logical_and(low, t == towers - 1), 0.0, value)
            put(x2, 144 * (r - 1), value.astype(BF16), tile)

    def second_block(at, mixed, tile):
        rows, lanes = mixed.shape[0], pl.ds(BINS * tile, BINS)
        value = grid1[pl.ds(C2 * (at + 1), rows), lanes] + mixed
        final[pl.ds(C2 * at, rows), lanes] = jnp.maximum(value, 0.0).astype(BF16)

    groups = ((0, 3), (3, 3), (6, 3), (9, 3), (12, 2), (14, 2))

    def tower(work):
        ones = [(tile, step, convolve(0, x1, 3 * step, 3, tile)) for tile, step in work if 0 <= step < 6]
        twos = [(tile, groups[step - 2], convolve(1, x2, *groups[step - 2], tile)) for tile, step in work if 2 <= step < 8]
        for tile, step in work:
            for r in range(3 * step + 5 if step >= 0 else 0, min(3 * step + 8, HEIGHT + 4) if step >= -1 else 0):
                pair_row(r, tile)
        ones = [(tile, step, remix(0, value)) for tile, step, value in ones]
        twos = [(tile, group, remix(1, value)) for tile, group, value in twos]
        for tile, step, value in ones:
            first_block(3 * step, value, tile)
        for tile, group, value in twos:
            second_block(group[0], value, tile)

    piece_copies = {}

    def piece_of(b, contact):
        start = STRIDE * b + first_row - (MOVED if b == 3 else 0)
        span = BINS if b < 2 else 128
        rows = []
        for r in range(HEIGHT):
            turned = pltpu.roll(contact[8 * r : 8 * r + 8], lax.rem(2 * BINS - r - start, BINS), 1)
            rows.append(turned[:, :span] * row_weights[b, r : r + 1, :span])
        return jnp.concatenate(rows, axis=0)

    def hand_on(b, piece):
        span = piece.shape[1]
        sent[b - 1, :, :span] = dot(squeeze[...], piece.astype(BF16)).astype(BF16)
        source = sent.at[b - 1, :, pl.ds(0, span)]
        target = landed.at[pl.ds(TARGETS * HEIGHT * (b - 1), TARGETS * HEIGHT), pl.ds(0, span)]
        piece_copies[b] = send(source, target, piece_send.at[b - 1], piece_recv.at[b - 1], at_genome(b))

    def contact_of(tile):
        return dot(wide_head[...], final[:, pl.ds(BINS * tile, BINS)])

    lags = (9,0,0)
    for moment in range(-1, lags[0] + 9):
        tower([(tile, moment - lags[tile]) for tile in (2, 1, 0)])
        if moment == lags[1] + 8:
            hand_on(1, piece_of(1, contact_of(1)))
            contact = contact_of(2)
            hand_on(3, piece_of(3, contact))
            hand_on(2, piece_of(2, contact))
    own_piece[...] = piece_of(0, contact_of(0))

    for b, copy in piece_copies.items():
        receive(copy, g >= b)
    rows = TARGETS * HEIGHT
    arrived = jnp.concatenate(
        [jnp.where(g >= b, landed[rows * (b - 1) : rows * b, :128].astype(F32), 0.0) for b in range(1, BLOCKS)], axis=0
    )
    near = own_piece[:, :128] + dot(expand[...], arrived.astype(BF16))
    arrived = jnp.where(g >= 1, landed[:rows, 128:].astype(F32), 0.0)
    near = [near[8 * r : 8 * r + 8] * row_weights[BLOCKS, r : r + 1, :128] for r in range(HEIGHT)]

    lane = iota((8, 128), 1)
    counted = jnp.logical_and(lane >= 1, lane <= STRIDE)
    joined = jnp.concatenate(near, axis=0)
    coarse = joined.astype(BF16)
    fine = (joined - coarse.astype(F32)).astype(BF16)
    squares = dot(jnp.concatenate([coarse, fine], axis=1), runs[...])
    insulation = upstream = downstream = jnp.zeros((8, 128), F32)
    for r in range(HEIGHT):
        insulation = insulation + pltpu.roll(squares[8 * r : 8 * r + 8], r, 1)
        contact = jnp.where(counted, jnp.exp(near[r]), 0.0)
        upstream = upstream + pltpu.roll(contact, r, 1)
        downstream = jnp.where(lane == r, jnp.sum(contact, axis=1, keepdims=True), downstream)
    part[0:8] = insulation
    part[8:16] = upstream
    part_copies = [
        send(part, parts_in.at[m - 1], part_send.at[m - 1], part_recv.at[m - 1], at_band(m)) for m in (3, 2, 4, 1)
    ]
    far = own_piece[:, 128:] + dot(expand[:, :rows], arrived.astype(BF16))
    for r in range(HEIGHT):
        band[:, r, :128] = near[r][:TARGETS]
        band[:, r, 128:] = (far[8 * r : 8 * r + 8] * row_weights[BLOCKS, r : r + 1, 128:])[:TARGETS]
    for m, copy in zip((3, 2, 4, 1), part_copies):
        receive(copy, place >= m)
    for m in range(1, BLOCKS + 1):
        turn = 128 - HEIGHT * m
        absent = float(HEIGHT) if m < BLOCKS else (HEIGHT - lane).astype(F32)
        insulation = insulation + jnp.where(place >= m, pltpu.roll(parts_in[m - 1, 0:8], turn, 1), 0.0)
        upstream = upstream + jnp.where(place >= m, pltpu.roll(parts_in[m - 1, 8:16], turn, 1), absent)
    scores[:, 0, :] = (insulation * (1.0 / (STRIDE * STRIDE)))[:TARGETS, :HEIGHT]
    scores[:, 1, :] = ((downstream - upstream) / (downstream + upstream))[:TARGETS, :HEIGHT]
    for copy, there in sends:

        @pl.when(there)
        def _():
            copy.wait_send()


def hand_over(band, scores, band_hbm, scores_hbm, sems):
    copies = [pltpu.make_async_copy(a, b, sems.at[i]) for i, (a, b) in enumerate(((band, band_hbm), (scores, scores_hbm)))]
    for copy in copies:
        copy.start()
    for copy in copies:
        copy.wait()


def solution(mesh):
    genomes, towers = mesh.shape["genome"], mesh.shape["tower"]

    def per_device(bases, stitch, stem, trunk_in, trunk_out, pair, rate, conv, mix, head):
        anywhere = pl.BlockSpec(memory_space=pl.ANY)
        vmem = pltpu.VMEM
        dma = pltpu.SemaphoreType.DMA
        many = 8 * HEIGHT
        shapes = (
            jax.ShapeDtypeStruct((TARGETS, HEIGHT, BINS), F32),
            jax.ShapeDtypeStruct((TARGETS, 2, HEIGHT), F32),
        )
        in_vmem = pl.BlockSpec(memory_space=pltpu.VMEM)
        results = pl.pallas_call(
            functools.partial(kernel, genomes, towers),
            out_shape=shapes,
            in_specs=[anywhere] * 10,
            out_specs=(in_vmem, in_vmem),
            scratch_shapes=[
                vmem((1024, 128), jnp.int32),
                vmem((1, BINS), jnp.int32),
                vmem((C1, 4 * BP), BF16),
                vmem((TRUNK, MID, 3 * C1), BF16),
                vmem((TRUNK, MID, C1), BF16),
                vmem((2 * C2, C1), BF16),
                vmem((1, C2), F32),
                vmem((2, 3, C2, 3 * C2), BF16),
                vmem((2, C2, C2), BF16),
                vmem((TARGETS, C2), BF16),
                vmem((BLOCKS, STRIDE, 128), BF16),
                vmem((TRUNK, 3 * MID, C1), BF16),
                vmem((TRUNK, C1, MID), BF16),
                vmem((2, 3 * C2, 15 * C2), BF16),
                vmem((2, 3 * C2, 3 * C2), BF16),
                vmem((many, HEIGHT * C2), BF16),
                vmem((3, 24, BINS), F32),
                vmem((C2, 128), F32),
                vmem((2 * 128, 128), BF16),
                vmem((BLOCKS + 1, HEIGHT, BINS), F32),
                vmem((C2, BINS), F32),
                vmem((2, C2, BINS), F32),
                vmem((20 * 144, 3 * BINS), BF16),
                vmem((18 * 144, 3 * BINS), BF16),
                vmem((18 * C2, 3 * BINS), F32),
                vmem((HEIGHT * C2, 3 * BINS), BF16),
                vmem((BLOCKS - 1, TARGETS * HEIGHT, BINS), BF16),
                vmem(((BLOCKS - 1) * TARGETS * HEIGHT, BINS), BF16),
                vmem((TARGETS * HEIGHT, many), BF16),
                vmem((many, 3 * TARGETS * HEIGHT), BF16),
                vmem((many, BINS), F32),
                vmem((16, 128), F32),
                vmem((BLOCKS, 16, 128), F32),
                dma((9,)),
                dma((CHUNKS,)),
                dma((BLOCKS - 1,)),
                dma((BLOCKS - 1,)),
                dma((BLOCKS - 1,)),
                dma((BLOCKS - 1,)),
                dma((BLOCKS,)),
                dma((BLOCKS,)),
            ],
            compiler_params=pltpu.CompilerParams(collective_id=0, has_side_effects=True),
            name="contacts",
        )(
            bases.reshape(-1, 128),
            stitch.reshape(1, -1),
            stem,
            trunk_in,
            jnp.swapaxes(trunk_out, 1, 2),
            pair,
            rate.reshape(1, -1),
            conv,
            mix,
            head,
        )
        band, scores = pl.pallas_call(
            hand_over,
            out_shape=shapes,
            in_specs=[in_vmem, in_vmem],
            out_specs=(anywhere, anywhere),
            scratch_shapes=[dma((2,))],
            name="hand_over",
        )(*results)
        return band, jnp.swapaxes(scores, 0, 1)

    placed = (P("genome"), P(), P(), P(), P(), P(), P(), P(), P(), P())
    return jax.shard_map(
        per_device,
        mesh=mesh,
        in_specs=placed,
        out_specs=(P(None, ("genome", "tower"), None), P(None, None, ("genome", "tower"))),
        check_vma=False,
    )
```
